128 devices in a mesh: query: 8 (over x, z_hi), tok: 16 (over y, z_lo, core).
Axes of the slice: x: 4, y: 4, z: 4 (z_hi: 2, z_lo: 2; z = z_hi * 2 + z_lo), core: 2. Of those that a mesh axis runs over, the one named last changes fastest.
Arguments:
- queries: bfloat16 [32768, 128], P('query'), may hold values from -16 to 16, as said below
- documents: bfloat16 [32768, 128], P('tok'), may hold values from -10 to 10, as said below
- cotangent: float32 [1024], P('query'), may hold values from -6 to 6
Outputs:
- grad_queries: float32 [32768, 128], P(('query', 'tok'))
- grad_documents: float32 [16, 2048, 128], P('tok', 'query')
The draws below stay inside these ranges and needn't reach their ends.
Inputs may be any that keep to these rules, and one draw needn't show every extreme that they name: `documents`: document embeddings of order one. `queries`: query embeddings of order one.
All inputs are finite; a program needn't handle non-finite values.
Results may differ from the reference program's by a relative error of at most 0.0029.
Values may be sent and summed in bfloat16 or wider, within the bound.
A program may use at most 64 MiB of HBM per device.

```python
import jax
import jax.numpy as jnp
from jax import lax

DIM = 128
QLEN = 32
DOC_DEV = 2048
QTOKENS = 32768
NQ = 1024
NDOC = 32768
N_TOK = 16


def doc_matrix(key):
    normal_key = jax.random.fold_in(key, 11)
    values = jax.random.normal(normal_key, (NDOC, DIM), jnp.float32)
    trend = 1.0 + 0.3 * jnp.arange(NDOC).astype(jnp.float32) / NDOC
    scale = 0.3 * trend
    return jnp.clip(values * scale[:, None], -10.0, 10.0)


def draw_documents(key, part):
    return doc_matrix(key).astype(jnp.bfloat16)


def draw_queries(key, part):
    value_key = jax.random.fold_in(key, 21)
    result = jnp.clip(0.35 * jax.random.normal(value_key, (QTOKENS, DIM), jnp.float32), -8.0, 8.0)
    return result.astype(jnp.bfloat16)


def block_scale(stream_key, dims, cuts, smallest, high):
    def one(axis_at, shards_of):
        draws = jax.random.uniform(jax.random.fold_in(jax.random.fold_in(stream_key, 6), axis_at), (shards_of,), jnp.float32, smallest / len(cuts), high / len(cuts))
        return jnp.repeat(jnp.exp(draws), dims[axis_at] // shards_of).reshape((-1,) + (1,) * (len(dims) - axis_at - 1))

    level = one(*cuts[0])
    for cut in cuts[1:]:
        level = level * one(*cut)
    return level


def centred(key, shape, width, reach, cuts=(), kind=jnp.bfloat16):
    entries = jax.random.normal(key, shape, jnp.float32) * width
    if len(cuts) > 0:
        entries = block_scale(key, shape, cuts, -0.22, 0.18) * entries
    return jnp.clip(entries, min=-reach, max=reach).astype(kind)


def setup_inputs(seed: int = 0) -> dict:
    key_of = jax.random.split(jax.random.key(seed), 4)
    return {
        "queries": draw_queries(jax.random.fold_in(key_of[3], 71), 0),
        "documents": draw_documents(jax.random.fold_in(key_of[3], 71), 0),
        "cotangent": centred(key_of[2], (NQ,), 1.0, 6.0, ((0, 8),), jnp.float32),
    }


inv_temp = 2.0


def reference(queries, documents, cotangent):
    blk_rows = min(512, QTOKENS)
    n_blocks = QTOKENS // blk_rows
    row_weight = jnp.broadcast_to(cotangent[:, None], (NQ, QLEN)).reshape(-1)
    q_blocks = queries.reshape(n_blocks, blk_rows, DIM)
    weight_blocks = row_weight.reshape(n_blocks, blk_rows)

    def one_block(doc_total, inputs_blk):
        q_rows, weight_rows = inputs_blk
        scores = jnp.dot(q_rows, documents.T, preferred_element_type=jnp.float32) * inv_temp
        row_top = jnp.max(scores, axis=1)
        log_total = row_top + jnp.log(jnp.sum(jnp.exp(scores - row_top[:, None]), axis=1))
        probs = jnp.exp(scores - log_total[:, None])
        weights_low = probs.astype(jnp.bfloat16)
        grad_rows = weight_rows[:, None] * jnp.dot(weights_low, documents, preferred_element_type=jnp.float32)
        scaled = (weight_rows[:, None] * probs).astype(jnp.bfloat16)
        doc_total = doc_total + jnp.dot(scaled.T, q_rows, preferred_element_type=jnp.float32)
        return doc_total, grad_rows

    doc_total, grad_blocks = lax.scan(one_block, jnp.zeros((NDOC, DIM), jnp.float32), (q_blocks, weight_blocks))
    return grad_blocks.reshape(QTOKENS, DIM), doc_total.reshape(N_TOK, DOC_DEV, DIM)
```

```python
import functools

import jax
import jax.numpy as jnp
from jax import lax
from jax.experimental import pallas as pl
from jax.experimental.pallas import tpu as pltpu
from jax.sharding import PartitionSpec as P

QLEN = 32
inv_temp = 2.0
LOG2E = 1.4426950408889634
SCALE = inv_temp * LOG2E

MESH = pl.DeviceIdType.MESH
F32 = jnp.float32
BF16 = jnp.bfloat16

BLK = 256
NBLK = 16
NDBLK = 8
DIM = 128
CHUNK = 256
NCHUNK = 8


def block_of(slot):
    half, rest = slot // 8, lax.rem(slot, 8)
    y, core = rest // 2, lax.rem(rest, 2)
    return 4 * y + 2 * lax.rem(half + y, 2) + core


def kernel(
    q_ref, d_ref, cot_ref, gq_ref, gd_ref,
    s_ref, u_ref, dc_ref, dt_ref, lse_mine, lse_all, lse_ref,
    pair_out, pair_in, part, q_out, q_in, d_out, d_in, d_own,
    lse_ss, lse_rs, pair_ss, pair_rs, q_ss, q_rs, d_ss, d_rs,
):
    qi, ti = lax.axis_index("query"), lax.axis_index("tok")
    x0, zh0 = qi // 2, lax.rem(qi, 2)
    y0, z0, core = ti // 4, lax.rem(ti // 2, 2), lax.rem(ti, 2)

    barrier = pltpu.get_barrier_semaphore()
    for k in range(1, 16):
        pl.semaphore_signal(barrier, inc=1, device_id=(qi, lax.rem(ti + k, 16)), device_id_type=MESH)
    for k in range(1, 8):
        pl.semaphore_signal(barrier, inc=1, device_id=(lax.rem(qi + k, 8), ti), device_id_type=MESH)

    for c in range(NCHUNK):
        rows = slice(c * CHUNK, (c + 1) * CHUNK)
        scaled = d_ref[rows, :].astype(F32) * SCALE
        high = scaled.astype(BF16)
        dc_ref[rows, 0:DIM] = high
        dc_ref[rows, DIM : 2 * DIM] = (scaled - high.astype(F32)).astype(BF16)

    def q_pair(slot):
        rows = q_ref[pl.ds(pl.multiple_of(block_of(slot) * BLK, BLK), BLK), :]
        return jnp.concatenate([rows, rows], axis=1)

    def score_chunk(slot, c, q2):
        rows = slice(c * CHUNK, (c + 1) * CHUNK)
        s = lax.dot_general(dc_ref[rows, :], q2, (((1,), (1,)), ((), ())), preferred_element_type=F32)
        s_ref[slot, rows, :] = s
        return jnp.max(s.reshape(CHUNK // 8, 8, BLK), axis=0)

    def exp_chunk(slot, c, top, total):
        e = jnp.exp2(s_ref[slot, slice(c * CHUNK, (c + 1) * CHUNK), :] - top)
        return total + jnp.sum(e.reshape(CHUNK // 8, 8, BLK), axis=0)

    def local_lse(half, row, top, total):
        lse_mine[half, pl.ds(row, 1), :] = top + jnp.log2(jnp.sum(total, axis=0, keepdims=True))

    def scores_of(slot):
        q2 = q_pair(slot)
        tops = score_chunk(slot, 0, q2)
        for c in range(1, NCHUNK):
            tops = jnp.maximum(tops, score_chunk(slot, c, q2))
        return tops

    def step_a(half):
        def body(slot, tops):
            cols = pl.ds(pl.multiple_of(slot * DIM, DIM), DIM)
            dt_ref[:, cols] = d_ref[cols, :].T
            top = jnp.max(tops, axis=0, keepdims=True)
            total = jnp.zeros((8, BLK), F32)
            q2 = q_pair(slot + 1)
            new = None
            for c in range(NCHUNK):
                total = exp_chunk(slot, c, top, total)
                t = score_chunk(slot + 1, c, q2)
                new = t if new is None else jnp.maximum(new, t)
            local_lse(half, slot - 8 * half, top, total)
            return new

        return body

    def lse_copy(half, k):
        return pltpu.make_async_remote_copy(
            src_ref=lse_mine.at[half], dst_ref=lse_all.at[half, k - 1],
            send_sem=lse_ss.at[half, k - 1], recv_sem=lse_rs.at[half, k - 1],
            device_id=(qi, lax.rem(ti + k, 16)), device_id_type=MESH,
        )

    tops = lax.fori_loop(0, 8, step_a(0), scores_of(0))
    pl.semaphore_wait(barrier, 22)
    for k in range(1, 16):
        lse_copy(0, k).start()
    tops = lax.fori_loop(8, 15, step_a(1), tops)
    cols = slice(15 * DIM, 16 * DIM)
    dt_ref[:, cols] = d_ref[cols, :].T
    top = jnp.max(tops, axis=0, keepdims=True)
    total = jnp.zeros((8, BLK), F32)
    for c in range(NCHUNK):
        total = exp_chunk(15, c, top, total)
    local_lse(1, 7, top, total)
    for k in range(1, 16):
        lse_copy(1, k).start()

    lane_query = lax.broadcasted_iota(jnp.int32, (1, BLK), 1) // QLEN

    def weights_of(block):
        w = jnp.zeros((1, BLK), F32)
        for g in range(BLK // QLEN):
            w = jnp.where(lane_query == g, cot_ref[block * (BLK // QLEN) + g], w)
        return w

    def probs_of(slot):
        lse = lse_ref[pl.ds(slot, 1), :]
        w = weights_of(block_of(slot))
        acc = jnp.zeros((DIM, BLK), F32)
        for c in range(NCHUNK):
            rows = slice(c * CHUNK, (c + 1) * CHUNK)
            p = jnp.exp2(s_ref[slot, rows, :] - lse)
            u_ref[slot, rows, :] = (w * p).astype(BF16)
            acc = acc + jnp.dot(dt_ref[:, rows], p.astype(BF16), preferred_element_type=F32)
        return (w * acc).T

    def pair_copy(st):
        return pltpu.make_async_remote_copy(
            src_ref=pair_out.at[st], dst_ref=pair_in.at[st],
            send_sem=pair_ss.at[st], recv_sem=pair_rs.at[st],
            device_id=(qi, ti + 1 - 2 * core), device_id_type=MESH,
        )

    def target(st):
        half, k = st // 4, lax.rem(st, 4)
        y = lax.rem(y0 + 1 + k, 4)
        return k, y, lax.rem(half + y, 2)

    def q_copy(st):
        k, y, z = target(st)
        slot = 2 * k + z0
        return pltpu.make_async_remote_copy(
            src_ref=q_out.at[st], dst_ref=q_in.at[slot],
            send_sem=q_ss.at[st], recv_sem=q_rs.at[slot],
            device_id=(qi, 4 * y + 2 * z + core), device_id_type=MESH,
        )

    def finish(st):
        pair_copy(st).wait_recv()
        both = part[st] + pair_in[st]
        part[st] = both
        q_out[st] = both.astype(BF16)

    def is_remote(st):
        k, y, z = target(st)
        return jnp.logical_or(k != 3, z != z0)

    def send(st):
        @pl.when(is_remote(st))
        def _():
            q_copy(st).start()

    def step_b(st, _):
        _, y, _ = target(st)
        base = 8 * (st // 4) + 2 * y
        pair_out[st] = probs_of(base + 1 - core)

        @pl.when(st > 0)
        def _():
            finish(st - 1)

        part[st] = probs_of(base + core)
        pair_copy(st).start()

        @pl.when(st > 0)
        def _():
            send(st - 1)

        return 0

    for half in range(2):
        for k in range(1, 16):
            lse_copy(half, k).wait_recv()
        top = lse_mine[half]
        for k in range(15):
            top = jnp.maximum(top, lse_all[half, k])
        total = jnp.exp2(lse_mine[half] - top)
        for k in range(15):
            total = total + jnp.exp2(lse_all[half, k] - top)
        lse_ref[8 * half : 8 * half + 8, :] = top + jnp.log2(total)
        lax.fori_loop(4 * half, 4 * half + 4, step_b, 0)

    def d_copy(m):
        x = lax.rem(x0 + lax.rem(m, 4) + 1, 4)
        zh = lax.rem(zh0 + 1 + m // 4, 2)
        return pltpu.make_async_remote_copy(
            src_ref=d_out.at[m], dst_ref=d_in.at[m],
            send_sem=d_ss.at[m], recv_sem=d_rs.at[m],
            device_id=(2 * x + zh, ti), device_id_type=MESH,
        )

    def docs_of(m):
        x = lax.rem(x0 + lax.rem(m, 4) + 1, 4)
        zh = lax.rem(zh0 + 1 + m // 4, 2)
        rows = pl.ds(pl.multiple_of((2 * x + zh) * BLK, BLK), BLK)
        acc = jnp.zeros((BLK, DIM), F32)
        for slot in range(NBLK):
            half, y, cb = slot // 8, (slot % 8) // 2, slot % 2
            blk = 4 * y + 2 * ((half + y) % 2) + cb
            acc = acc + jnp.dot(
                u_ref[slot, rows, :], q_ref[blk * BLK : (blk + 1) * BLK, :], preferred_element_type=F32
            )
        return acc

    def step_c(m, _):
        d_out[m] = docs_of(m).astype(BF16)
        d_copy(m).start()
        return 0

    finish(7)
    send(7)
    lax.fori_loop(0, 7, step_c, 0)
    d_own[...] = docs_of(7)

    mine = jnp.where(lax.rem(y0 + z0, 2) == 0, 3, 7)
    gq_ref[...] = part[mine]
    for k in range(4):
        for z in range(2):
            slot = 2 * k + z

            def add(slot=slot):
                q_copy_in = pltpu.make_async_remote_copy(
                    src_ref=q_out.at[0], dst_ref=q_in.at[slot],
                    send_sem=q_ss.at[0], recv_sem=q_rs.at[slot],
                    device_id=(qi, lax.rem(ti + 2, 16)), device_id_type=MESH,
                )
                q_copy_in.wait_recv()
                gq_ref[...] += q_in[slot].astype(F32)

            if k < 3:
                add()
            else:
                pl.when(z != z0)(add)
    total = d_own[...]
    for m in range(7):
        d_copy(m).wait_recv()
        total = total + d_in[m].astype(F32)
    gd_ref[0] = total

    for half in range(2):
        for k in range(1, 16):
            lse_copy(half, k).wait_send()
    for st in range(8):
        pair_copy(st).wait_send()

        @pl.when(is_remote(st))
        def _():
            q_copy(st).wait_send()

    for m in range(7):
        d_copy(m).wait_send()


def shards(queries, documents, cotangent):
    vmem = pl.BlockSpec(memory_space=pltpu.VMEM)
    dma = pltpu.SemaphoreType.DMA
    n_docs = documents.shape[0]
    return pl.pallas_call(
        kernel,
        out_shape=(
            jax.ShapeDtypeStruct((BLK, DIM), F32),
            jax.ShapeDtypeStruct((1, BLK, DIM), F32),
        ),
        in_specs=[vmem, vmem, pl.BlockSpec(memory_space=pltpu.SMEM)],
        out_specs=(vmem, vmem),
        scratch_shapes=[
            pltpu.VMEM((NBLK, n_docs, BLK), F32),
            pltpu.VMEM((NBLK, n_docs, BLK), BF16),
            pltpu.VMEM((n_docs, 2 * DIM), BF16),
            pltpu.VMEM((DIM, n_docs), BF16),
            pltpu.VMEM((2, 8, BLK), F32),
            pltpu.VMEM((2, 15, 8, BLK), F32),
            pltpu.VMEM((NBLK, BLK), F32),
            pltpu.VMEM((8, BLK, DIM), F32),
            pltpu.VMEM((8, BLK, DIM), F32),
            pltpu.VMEM((8, BLK, DIM), F32),
            pltpu.VMEM((8, BLK, DIM), BF16),
            pltpu.VMEM((8, BLK, DIM), BF16),
            pltpu.VMEM((7, BLK, DIM), BF16),
            pltpu.VMEM((7, BLK, DIM), BF16),
            pltpu.VMEM((BLK, DIM), F32),
            dma((2, 15)), dma((2, 15)), dma((8,)), dma((8,)),
            dma((8,)), dma((8,)), dma((7,)), dma((7,)),
        ],
        compiler_params=pltpu.CompilerParams(
            collective_id=0, has_side_effects=True, vmem_limit_bytes=67043328
        ),
    )(queries, documents, cotangent)


def solution(mesh):
    placed = (P("query", None), P("tok", None), P("query"))
    return jax.shard_map(
        shards,
        mesh=mesh,
        in_specs=placed,
        out_specs=(P(("query", "tok"), None), P("tok", "query", None)),
        check_vma=False,
    )
```

```python
import functools

import jax
import jax.numpy as jnp
from jax import lax
from jax.experimental import pallas as pl
from jax.experimental.pallas import tpu as pltpu
from jax.sharding import PartitionSpec as P

QLEN = 32
inv_temp = 2.0
LOG2E = 1.4426950408889634
SCALE = inv_temp * LOG2E

MESH = pl.DeviceIdType.MESH
F32 = jnp.float32
BF16 = jnp.bfloat16

BLK = 256
NBLK = 16
NDBLK = 8
DIM = 128
CHUNK = 256
NCHUNK = 8
SUBROWS = 16


def block_of(slot):
    half, rest = slot // 8, lax.rem(slot, 8)
    y, core = rest // 2, lax.rem(rest, 2)
    return 4 * y + 2 * lax.rem(half + y, 2) + core


def kernel(
    q_ref, d_ref, cot_ref, gq_ref, gd_ref,
    s_ref, u_ref, dc_ref, dt_ref, lse_mine, lse_all, lse_ref,
    pair_out, pair_in, part, q_out, q_in, d_out, d_in, d_own,
    lse_ss, lse_rs, pair_ss, pair_rs, q_ss, q_rs, d_ss, d_rs,
):
    qi, ti = lax.axis_index("query"), lax.axis_index("tok")
    x0, zh0 = qi // 2, lax.rem(qi, 2)
    y0, z0, core = ti // 4, lax.rem(ti // 2, 2), lax.rem(ti, 2)

    barrier = pltpu.get_barrier_semaphore()
    for k in range(1, 16):
        pl.semaphore_signal(barrier, inc=1, device_id=(qi, lax.rem(ti + k, 16)), device_id_type=MESH)
    for k in range(1, 8):
        pl.semaphore_signal(barrier, inc=1, device_id=(lax.rem(qi + k, 8), ti), device_id_type=MESH)

    for c in range(NCHUNK):
        rows = slice(c * CHUNK, (c + 1) * CHUNK)
        scaled = d_ref[rows, :].astype(F32) * SCALE
        high = scaled.astype(BF16)
        dc_ref[rows, 0:DIM] = high
        dc_ref[rows, DIM : 2 * DIM] = (scaled - high.astype(F32)).astype(BF16)

    def q_pair(slot):
        rows = q_ref[pl.ds(pl.multiple_of(block_of(slot) * BLK, BLK), BLK), :]
        return jnp.concatenate([rows, rows], axis=1)

    def score_chunk(slot, c, q2, tops):
        rows = slice(c * CHUNK, (c + 1) * CHUNK)
        s = lax.dot_general(dc_ref[rows, :], q2, (((1,), (1,)), ((), ())), preferred_element_type=F32)
        s_ref[slot, rows, :] = s
        for i in range(0, CHUNK, SUBROWS):
            part_s = s[i : i + SUBROWS]
            tops = part_s if tops is None else jnp.maximum(tops, part_s)
        return tops

    def exp_chunk(slot, c, top, total):
        for i in range(c * CHUNK, (c + 1) * CHUNK, SUBROWS):
            e = jnp.exp2(s_ref[slot, i : i + SUBROWS, :] - top)
            total = e if total is None else total + e
        return total

    def local_lse(half, row, top, total):
        lse_mine[half, pl.ds(row, 1), :] = top + jnp.log2(jnp.sum(total, axis=0, keepdims=True))

    def scores_of(slot):
        q2 = q_pair(slot)
        tops = None
        for c in range(NCHUNK):
            tops = score_chunk(slot, c, q2, tops)
        return jnp.max(tops, axis=0, keepdims=True)

    def turn(i):
        cols = pl.ds(pl.multiple_of(i * 2 * DIM, 2 * DIM), 2 * DIM)
        dt_ref[:, cols] = d_ref[cols, :].T

    def step_a(half):
        def body(i, tops):
            turn(i)
            new = []
            for k in range(2):
                slot = 2 * i + k
                q2 = q_pair(slot + 2)
                total = fresh = None
                for c in range(NCHUNK):
                    total = exp_chunk(slot, c, tops[k], total)
                    fresh = score_chunk(slot + 2, c, q2, fresh)
                local_lse(half, slot - 8 * half, tops[k], total)
                new.append(jnp.max(fresh, axis=0, keepdims=True))
            return tuple(new)

        return body

    def lse_copy(half, k):
        return pltpu.make_async_remote_copy(
            src_ref=lse_mine.at[half], dst_ref=lse_all.at[half, k - 1],
            send_sem=lse_ss.at[half, k - 1], recv_sem=lse_rs.at[half, k - 1],
            device_id=(qi, lax.rem(ti + k, 16)), device_id_type=MESH,
        )

    tops = lax.fori_loop(0, 4, step_a(0), (scores_of(0), scores_of(1)))
    pl.semaphore_wait(barrier, 22)
    for k in range(1, 16):
        lse_copy(0, k).start()
    tops = lax.fori_loop(4, 7, step_a(1), tops)
    turn(7)
    for k in range(2):
        total = None
        for c in range(NCHUNK):
            total = exp_chunk(14 + k, c, tops[k], total)
        local_lse(1, 6 + k, tops[k], total)
    for k in range(1, 16):
        lse_copy(1, k).start()

    lane_query = lax.broadcasted_iota(jnp.int32, (1, BLK), 1) // QLEN

    def weights_of(block):
        w = jnp.zeros((1, BLK), F32)
        for g in range(BLK // QLEN):
            w = jnp.where(lane_query == g, cot_ref[block * (BLK // QLEN) + g], w)
        return w

    def probs_of(slot):
        lse = lse_ref[pl.ds(slot, 1), :]
        w = weights_of(block_of(slot))
        acc = jnp.zeros((DIM, BLK), F32)
        for c in range(NCHUNK):
            rows = slice(c * CHUNK, (c + 1) * CHUNK)
            p = jnp.exp2(s_ref[slot, rows, :] - lse)
            u_ref[slot, rows, :] = (w * p).astype(BF16)
            acc = acc + jnp.dot(dt_ref[:, rows], p.astype(BF16), preferred_element_type=F32)
        return (w * acc).T

    def pair_copy(st):
        return pltpu.make_async_remote_copy(
            src_ref=pair_out.at[st], dst_ref=pair_in.at[st],
            send_sem=pair_ss.at[st], recv_sem=pair_rs.at[st],
            device_id=(qi, ti + 1 - 2 * core), device_id_type=MESH,
        )

    def target(st):
        half, k = st // 4, lax.rem(st, 4)
        y = lax.rem(y0 + 1 + k, 4)
        return k, y, lax.rem(half + y, 2)

    def q_copy(st):
        k, y, z = target(st)
        slot = 2 * k + z0
        return pltpu.make_async_remote_copy(
            src_ref=q_out.at[st], dst_ref=q_in.at[slot],
            send_sem=q_ss.at[st], recv_sem=q_rs.at[slot],
            device_id=(qi, 4 * y + 2 * z + core), device_id_type=MESH,
        )

    def finish(st):
        pair_copy(st).wait_recv()
        both = part[st] + pair_in[st]
        part[st] = both
        q_out[st] = both.astype(BF16)

    def is_remote(st):
        k, y, z = target(st)
        return jnp.logical_or(k != 3, z != z0)

    def send(st):
        @pl.when(is_remote(st))
        def _():
            q_copy(st).start()

    def step_b(i, _):
        for st in (2 * i, 2 * i + 1):
            _, y, _ = target(st)
            base = 8 * (st // 4) + 2 * y
            pair_out[st] = probs_of(base + 1 - core)
            part[st] = probs_of(base + core)
        for st in (2 * i, 2 * i + 1):
            pair_copy(st).start()

        @pl.when(i > 0)
        def _():
            for st in (2 * i - 2, 2 * i - 1):
                finish(st)
            for st in (2 * i - 2, 2 * i - 1):
                send(st)

        return 0

    for half in range(2):
        for k in range(1, 16):
            lse_copy(half, k).wait_recv()
        top = lse_mine[half]
        for k in range(15):
            top = jnp.maximum(top, lse_all[half, k])
        total = jnp.exp2(lse_mine[half] - top)
        for k in range(15):
            total = total + jnp.exp2(lse_all[half, k] - top)
        lse_ref[8 * half : 8 * half + 8, :] = top + jnp.log2(total)
        lax.fori_loop(2 * half, 2 * half + 2, step_b, 0)

    def d_copy(m):
        x = lax.rem(x0 + lax.rem(m, 4) + 1, 4)
        zh = lax.rem(zh0 + 1 + m // 4, 2)
        return pltpu.make_async_remote_copy(
            src_ref=d_out.at[m], dst_ref=d_in.at[m],
            send_sem=d_ss.at[m], recv_sem=d_rs.at[m],
            device_id=(2 * x + zh, ti), device_id_type=MESH,
        )

    def docs_of(m):
        x = lax.rem(x0 + lax.rem(m, 4) + 1, 4)
        zh = lax.rem(zh0 + 1 + m // 4, 2)
        rows = pl.ds(pl.multiple_of((2 * x + zh) * BLK, BLK), BLK)
        acc = jnp.zeros((BLK, DIM), F32)
        for slot in range(NBLK):
            half, y, cb = slot // 8, (slot % 8) // 2, slot % 2
            blk = 4 * y + 2 * ((half + y) % 2) + cb
            acc = acc + jnp.dot(
                u_ref[slot, rows, :], q_ref[blk * BLK : (blk + 1) * BLK, :], preferred_element_type=F32
            )
        return acc

    def step_c(m, _):
        d_out[m] = docs_of(m).astype(BF16)
        d_copy(m).start()
        return 0

    lax.fori_loop(0, 1, step_c, 0)
    for st in (6, 7):
        finish(st)
    for st in (6, 7):
        send(st)
    lax.fori_loop(1, 7, step_c, 0)
    d_own[...] = docs_of(7)

    mine = jnp.where(lax.rem(y0 + z0, 2) == 0, 3, 7)
    gq_ref[...] = part[mine]
    for k in range(4):
        for z in range(2):
            slot = 2 * k + z

            def add(slot=slot):
                q_copy_in = pltpu.make_async_remote_copy(
                    src_ref=q_out.at[0], dst_ref=q_in.at[slot],
                    send_sem=q_ss.at[0], recv_sem=q_rs.at[slot],
                    device_id=(qi, lax.rem(ti + 2, 16)), device_id_type=MESH,
                )
                q_copy_in.wait_recv()
                gq_ref[...] += q_in[slot].astype(F32)

            if k < 3:
                add()
            else:
                pl.when(z != z0)(add)
    total = d_own[...]
    for m in range(7):
        d_copy(m).wait_recv()
        total = total + d_in[m].astype(F32)
    gd_ref[0] = total

    for half in range(2):
        for k in range(1, 16):
            lse_copy(half, k).wait_send()
    for st in range(8):
        pair_copy(st).wait_send()

        @pl.when(is_remote(st))
        def _():
            q_copy(st).wait_send()

    for m in range(7):
        d_copy(m).wait_send()


def shards(queries, documents, cotangent):
    vmem = pl.BlockSpec(memory_space=pltpu.VMEM)
    dma = pltpu.SemaphoreType.DMA
    n_docs = documents.shape[0]
    return pl.pallas_call(
        kernel,
        out_shape=(
            jax.ShapeDtypeStruct((BLK, DIM), F32),
            jax.ShapeDtypeStruct((1, BLK, DIM), F32),
        ),
        in_specs=[vmem, vmem, pl.BlockSpec(memory_space=pltpu.SMEM)],
        out_specs=(vmem, vmem),
        scratch_shapes=[
            pltpu.VMEM((NBLK, n_docs, BLK), F32),
            pltpu.VMEM((NBLK, n_docs, BLK), BF16),
            pltpu.VMEM((n_docs, 2 * DIM), BF16),
            pltpu.VMEM((DIM, n_docs), BF16),
            pltpu.VMEM((2, 8, BLK), F32),
            pltpu.VMEM((2, 15, 8, BLK), F32),
            pltpu.VMEM((NBLK, BLK), F32),
            pltpu.VMEM((8, BLK, DIM), F32),
            pltpu.VMEM((8, BLK, DIM), F32),
            pltpu.VMEM((8, BLK, DIM), F32),
            pltpu.VMEM((8, BLK, DIM), BF16),
            pltpu.VMEM((8, BLK, DIM), BF16),
            pltpu.VMEM((7, BLK, DIM), BF16),
            pltpu.VMEM((7, BLK, DIM), BF16),
            pltpu.VMEM((BLK, DIM), F32),
            dma((2, 15)), dma((2, 15)), dma((8,)), dma((8,)),
            dma((8,)), dma((8,)), dma((7,)), dma((7,)),
        ],
        compiler_params=pltpu.CompilerParams(
            collective_id=0, has_side_effects=True, vmem_limit_bytes=67043328
        ),
    )(queries, documents, cotangent)


def solution(mesh):
    placed = (P("query", None), P("tok", None), P("query"))
    return jax.shard_map(
        shards,
        mesh=mesh,
        in_specs=placed,
        out_specs=(P(("query", "tok"), None), P("tok", "query", None)),
        check_vma=False,
    )
```

```python
import functools

import jax
import jax.numpy as jnp
from jax import lax
from jax.experimental import pallas as pl
from jax.experimental.pallas import tpu as pltpu
from jax.sharding import PartitionSpec as P

QLEN = 32
inv_temp = 2.0
LOG2E = 1.4426950408889634
SCALE = inv_temp * LOG2E

MESH = pl.DeviceIdType.MESH
F32 = jnp.float32
BF16 = jnp.bfloat16

BLK = 256
NBLK = 16
NDBLK = 8
DIM = 128
CHUNK = 256
NCHUNK = 8
SUBROWS = 16


def static_block(slot):
    half, y, core = slot // 8, (slot % 8) // 2, slot % 2
    return 4 * y + 2 * ((half + y) % 2) + core


def block_of(slot):
    half, rest = slot // 8, lax.rem(slot, 8)
    y, core = rest // 2, lax.rem(rest, 2)
    return 4 * y + 2 * lax.rem(half + y, 2) + core


def kernel(
    q_ref, d_ref, cot_ref, gq_ref, gd_ref,
    s_ref, dc_ref, dt_ref, w_ref, lse_mine, lse_all, lse_ref,
    pair_out, pair_in, part, q_out, q_in, d_part, d_out, d_in,
    lse_ss, lse_rs, pair_ss, pair_rs, q_ss, q_rs, d_ss, d_rs,
):
    qi, ti = lax.axis_index("query"), lax.axis_index("tok")
    x0, zh0 = qi // 2, lax.rem(qi, 2)
    y0, z0, core = ti // 4, lax.rem(ti // 2, 2), lax.rem(ti, 2)

    barrier = pltpu.get_barrier_semaphore()
    for k in range(1, 16):
        pl.semaphore_signal(barrier, inc=1, device_id=(qi, lax.rem(ti + k, 16)), device_id_type=MESH)
    for k in range(1, 8):
        pl.semaphore_signal(barrier, inc=1, device_id=(lax.rem(qi + k, 8), ti), device_id_type=MESH)

    for c in range(NCHUNK):
        rows = slice(c * CHUNK, (c + 1) * CHUNK)
        scaled = d_ref[rows, :].astype(F32) * SCALE
        high = scaled.astype(BF16)
        dc_ref[rows, 0:DIM] = high
        dc_ref[rows, DIM : 2 * DIM] = (scaled - high.astype(F32)).astype(BF16)
        dt_ref[:, rows] = d_ref[rows, :].T

    def target(st):
        half, k = st // 4, lax.rem(st, 4)
        y = lax.rem(y0 + 1 + k, 4)
        return k, y, lax.rem(half + y, 2)

    def slots_of(st):
        _, y, _ = target(st)
        base = 8 * (st // 4) + 2 * y
        return base + 1 - core, base + core

    def q_pair(slot):
        rows = q_ref[pl.ds(pl.multiple_of(block_of(slot) * BLK, BLK), BLK), :]
        return jnp.concatenate([rows, rows], axis=1)

    def score_chunk(slot, c, q2, tops):
        rows = slice(c * CHUNK, (c + 1) * CHUNK)
        s = lax.dot_general(dc_ref[rows, :], q2, (((1,), (1,)), ((), ())), preferred_element_type=F32)
        s_ref[slot, rows, :] = s
        for i in range(0, CHUNK, SUBROWS):
            part_s = s[i : i + SUBROWS]
            tops = part_s if tops is None else jnp.maximum(tops, part_s)
        return tops

    def scores_of(slot):
        q2 = q_pair(slot)
        tops = None
        for c in range(NCHUNK):
            tops = score_chunk(slot, c, q2, tops)
        return jnp.max(tops, axis=0, keepdims=True)

    def step_a(st, tops, half, more):
        new = []
        slots = slots_of(st)
        following = slots_of(st + 1)
        for k in range(2):
            slot = slots[k]
            q2 = q_pair(following[k]) if more else None
            total = fresh = None
            acc = jnp.zeros((DIM, BLK), F32)
            for c in range(NCHUNK):
                rows = slice(c * CHUNK, (c + 1) * CHUNK)
                e = jnp.exp2(s_ref[slot, rows, :] - tops[k])
                for i in range(0, CHUNK, SUBROWS):
                    part_e = e[i : i + SUBROWS]
                    total = part_e if total is None else total + part_e
                acc = acc + jnp.dot(dt_ref[:, rows], e.astype(BF16), preferred_element_type=F32)
                if more:
                    fresh = score_chunk(following[k], c, q2, fresh)
            total = jnp.sum(total, axis=0, keepdims=True)
            lse = tops[k] + jnp.log2(total)
            lse_mine[half, pl.ds(slot - 8 * half, 1), :] = lse
            mean = acc * (1.0 / total)
            if k == 0:
                pair_out[st, 0:DIM, :] = mean
                pair_out[st, DIM : DIM + 8, :] = jnp.broadcast_to(lse, (8, BLK))
            else:
                part[st] = mean
            if more:
                new.append(jnp.max(fresh, axis=0, keepdims=True))
        return tuple(new)

    def lse_copy(half, k):
        return pltpu.make_async_remote_copy(
            src_ref=lse_mine.at[half], dst_ref=lse_all.at[half, k - 1],
            send_sem=lse_ss.at[half, k - 1], recv_sem=lse_rs.at[half, k - 1],
            device_id=(qi, lax.rem(ti + k, 16)), device_id_type=MESH,
        )

    def pair_copy(st):
        return pltpu.make_async_remote_copy(
            src_ref=pair_out.at[st], dst_ref=pair_in.at[st],
            send_sem=pair_ss.at[st], recv_sem=pair_rs.at[st],
            device_id=(qi, ti + 1 - 2 * core), device_id_type=MESH,
        )

    def q_copy(st):
        k, y, z = target(st)
        slot = 2 * k + z0
        return pltpu.make_async_remote_copy(
            src_ref=q_out.at[st], dst_ref=q_in.at[slot],
            send_sem=q_ss.at[st], recv_sem=q_rs.at[slot],
            device_id=(qi, 4 * y + 2 * z + core), device_id_type=MESH,
        )

    def finish(st, half):
        pair_copy(st).wait_recv()
        mine = lse_mine[half, pl.ds(slots_of(st)[1] - 8 * half, 1), :]
        theirs = pair_in[st, DIM : DIM + 1, :]
        top = jnp.maximum(mine, theirs)
        a, b = jnp.exp2(mine - top), jnp.exp2(theirs - top)
        scale = 1.0 / (a + b)
        both = part[st] * (a * scale) + pair_in[st, 0:DIM, :] * (b * scale)
        part[st] = both
        q_out[st] = both.astype(BF16)

    def is_remote(st):
        k, _, z = target(st)
        return jnp.logical_or(k != 3, z != z0)

    def send(st):
        @pl.when(is_remote(st))
        def _():
            q_copy(st).start()

    first = slots_of(0)
    tops = lax.fori_loop(
        0, 4, lambda st, tops: step_a(st, tops, 0, True), (scores_of(first[0]), scores_of(first[1]))
    )
    pl.semaphore_wait(barrier, 22)
    for k in range(1, 16):
        lse_copy(0, k).start()
    for st in range(4):
        pair_copy(st).start()

    def second(st, tops):
        tops = step_a(st, tops, 1, True)
        finish(st - 4, 0)
        pair_copy(st).start()
        send(st - 4)
        return tops

    tops = lax.fori_loop(4, 7, second, tops)
    step_a(7, tops, 1, False)
    for k in range(1, 16):
        lse_copy(1, k).start()
    pair_copy(7).start()

    lane_query = lax.broadcasted_iota(jnp.int32, (1, BLK), 1) // QLEN
    for slot in range(NBLK):
        w = jnp.zeros((1, BLK), F32)
        for g in range(BLK // QLEN):
            w = jnp.where(lane_query == g, cot_ref[static_block(slot) * (BLK // QLEN) + g], w)
        w_ref[slot : slot + 1, :] = w
    finish(3, 0)
    send(3)
    for st in range(4, 7):
        finish(st, 1)
        send(st)

    def global_lse(half):
        for k in range(1, 16):
            lse_copy(half, k).wait_recv()
        top = lse_mine[half]
        for k in range(15):
            top = jnp.maximum(top, lse_all[half, k])
        total = jnp.exp2(lse_mine[half] - top)
        for k in range(15):
            total = total + jnp.exp2(lse_all[half, k] - top)
        lse_ref[8 * half : 8 * half + 8, :] = top + jnp.log2(total)

    def d_target(m):
        x = lax.rem(x0 + lax.rem(m, 4) + 1, 4)
        zh = lax.rem(zh0 + 1 + m // 4, 2)
        return 2 * x + zh

    def d_copy(m):
        return pltpu.make_async_remote_copy(
            src_ref=d_out.at[m], dst_ref=d_in.at[m],
            send_sem=d_ss.at[m], recv_sem=d_rs.at[m],
            device_id=(d_target(m), ti), device_id_type=MESH,
        )

    def docs_of(m, half, acc):
        rows = pl.ds(pl.multiple_of(d_target(m) * BLK, BLK), BLK)
        for slot in range(8 * half, 8 * half + 8):
            blk = static_block(slot)
            p = jnp.exp2(s_ref[slot, rows, :] - lse_ref[slot : slot + 1, :])
            u = (w_ref[slot : slot + 1, :] * p).astype(BF16)
            acc = acc + jnp.dot(u, q_ref[blk * BLK : (blk + 1) * BLK, :], preferred_element_type=F32)
        return acc

    def early(i, _):
        for m in (2 * i, 2 * i + 1):
            d_part[m] = docs_of(m, 0, jnp.zeros((BLK, DIM), F32))
        return 0

    global_lse(0)
    lax.fori_loop(0, 4, early, 0)
    finish(7, 1)
    send(7)
    global_lse(1)

    def late(m, _):
        d_out[m] = docs_of(m, 1, d_part[m]).astype(BF16)
        d_copy(m).start()
        return 0

    lax.fori_loop(0, 7, late, 0)
    d_part[7] = docs_of(7, 1, d_part[7])

    own_half = lax.rem(y0 + z0, 2)
    row = pl.ds(2 * y0 + core, 1)
    lse = lse_ref[pl.ds(8 * own_half + 2 * y0 + core, 1), :]

    def share(ys, zs):
        both = jnp.zeros((1, BLK), F32)
        for cs in range(2):
            k = lax.rem(ti - (4 * ys + 2 * zs + cs) + 16, 16)
            both = both + jnp.exp2(lse_all[own_half, k - 1, row, :] - lse)
        return both

    partner = jnp.where(core == 1, 0, 14)
    own_share = jnp.exp2(lse_mine[own_half, row, :] - lse) + jnp.exp2(lse_all[own_half, partner, row, :] - lse)
    own_step = jnp.where(own_half == 0, 3, 7)
    part[0] = part[own_step] * own_share
    for k in range(4):
        for z in range(2):
            slot = 2 * k + z

            def add(k=k, z=z, slot=slot):
                pltpu.make_async_remote_copy(
                    src_ref=q_out.at[0], dst_ref=q_in.at[slot],
                    send_sem=q_ss.at[0], recv_sem=q_rs.at[slot],
                    device_id=(qi, lax.rem(ti + 2, 16)), device_id_type=MESH,
                ).wait_recv()
                part[0] += q_in[slot].astype(F32) * share(lax.rem(y0 + 3 - k, 4), z)

            if k < 3:
                add()
            else:
                pl.when(z != z0)(add)
    gq_ref[...] = (part[0] * w_ref[pl.ds(8 * own_half + 2 * y0 + core, 1), :]).T
    total = d_part[7]
    for m in range(7):
        d_copy(m).wait_recv()
        total = total + d_in[m].astype(F32)
    gd_ref[0] = total

    for half in range(2):
        for k in range(1, 16):
            lse_copy(half, k).wait_send()
    for st in range(8):
        pair_copy(st).wait_send()

        @pl.when(is_remote(st))
        def _():
            q_copy(st).wait_send()

    for m in range(7):
        d_copy(m).wait_send()


def shards(queries, documents, cotangent):
    vmem = pl.BlockSpec(memory_space=pltpu.VMEM)
    dma = pltpu.SemaphoreType.DMA
    n_docs = documents.shape[0]
    return pl.pallas_call(
        kernel,
        out_shape=(
            jax.ShapeDtypeStruct((BLK, DIM), F32),
            jax.ShapeDtypeStruct((1, BLK, DIM), F32),
        ),
        in_specs=[vmem, vmem, pl.BlockSpec(memory_space=pltpu.SMEM)],
        out_specs=(vmem, vmem),
        scratch_shapes=[
            pltpu.VMEM((NBLK, n_docs, BLK), F32),
            pltpu.VMEM((n_docs, 2 * DIM), BF16),
            pltpu.VMEM((DIM, n_docs), BF16),
            pltpu.VMEM((NBLK, BLK), F32),
            pltpu.VMEM((2, 8, BLK), F32),
            pltpu.VMEM((2, 15, 8, BLK), F32),
            pltpu.VMEM((NBLK, BLK), F32),
            pltpu.VMEM((8, DIM + 8, BLK), F32),
            pltpu.VMEM((8, DIM + 8, BLK), F32),
            pltpu.VMEM((8, DIM, BLK), F32),
            pltpu.VMEM((8, DIM, BLK), BF16),
            pltpu.VMEM((8, DIM, BLK), BF16),
            pltpu.VMEM((8, BLK, DIM), F32),
            pltpu.VMEM((7, BLK, DIM), BF16),
            pltpu.VMEM((7, BLK, DIM), BF16),
            dma((2, 15)), dma((2, 15)), dma((8,)), dma((8,)),
            dma((8,)), dma((8,)), dma((7,)), dma((7,)),
        ],
        compiler_params=pltpu.CompilerParams(
            collective_id=0, has_side_effects=True, vmem_limit_bytes=67043328
        ),
    )(queries, documents, cotangent)


def solution(mesh):
    placed = (P("query", None), P("tok", None), P("query"))
    return jax.shard_map(
        shards,
        mesh=mesh,
        in_specs=placed,
        out_specs=(P(("query", "tok"), None), P("tok", "query", None)),
        check_vma=False,
    )
```

```python
import functools

import jax
import jax.numpy as jnp
from jax import lax
from jax.experimental import pallas as pl
from jax.experimental.pallas import tpu as pltpu
from jax.sharding import PartitionSpec as P

QLEN = 32
inv_temp = 2.0
LOG2E = 1.4426950408889634
SCALE = inv_temp * LOG2E

MESH = pl.DeviceIdType.MESH
F32 = jnp.float32
BF16 = jnp.bfloat16

BLK = 256
NBLK = 16
NDBLK = 8
DIM = 128
CHUNK = 256
NCHUNK = 8
SUBROWS = 16
Z_COPY = None


def block_of(slot):
    half, rest = slot // 8, lax.rem(slot, 8)
    y, core = rest // 2, lax.rem(rest, 2)
    return 4 * y + 2 * lax.rem(half + y, 2) + core


def kernel(
    q_ref, d_ref, cot_ref, gq_ref, gd_ref,
    s_ref, u_ref, dc_ref, dt_ref, acc_ref, w_ref, lse_mine, lse_all, lse_ref,
    pair_out, pair_in, part, q_out, q_in, d_out, d_in, d_own,
    lse_ss, lse_rs, pair_ss, pair_rs, q_ss, q_rs, d_ss, d_rs,
):
    qi, ti = lax.axis_index("query"), lax.axis_index("tok")
    x0, zh0 = qi // 2, lax.rem(qi, 2)
    y0, z0, core = ti // 4, lax.rem(ti // 2, 2), lax.rem(ti, 2)

    barrier = pltpu.get_barrier_semaphore()
    for k in range(1, 16):
        pl.semaphore_signal(barrier, inc=1, device_id=(qi, lax.rem(ti + k, 16)), device_id_type=MESH)
    for k in range(1, 4):
        pl.semaphore_signal(barrier, inc=1, device_id=(2 * lax.rem(x0 + k, 4) + zh0, ti), device_id_type=MESH)
    pl.semaphore_signal(barrier, inc=1, device_id=(2 * x0 + 1 - zh0, ti), device_id_type=MESH)

    for c in range(NCHUNK):
        rows = slice(c * CHUNK, (c + 1) * CHUNK)
        scaled = d_ref[rows, :].astype(F32) * SCALE
        high = scaled.astype(BF16)
        dc_ref[rows, 0:DIM] = high
        dc_ref[rows, DIM : 2 * DIM] = (scaled - high.astype(F32)).astype(BF16)

    def q_pair(slot):
        rows = q_ref[pl.ds(pl.multiple_of(block_of(slot) * BLK, BLK), BLK), :]
        return jnp.concatenate([rows, rows], axis=1)

    def score_chunk(slot, c, q2, tops):
        rows = slice(c * CHUNK, (c + 1) * CHUNK)
        s = lax.dot_general(dc_ref[rows, :], q2, (((1,), (1,)), ((), ())), preferred_element_type=F32)
        s_ref[slot, rows, :] = s
        for i in range(0, CHUNK, SUBROWS):
            part_s = s[i : i + SUBROWS]
            tops = part_s if tops is None else jnp.maximum(tops, part_s)
        return tops

    def exp_chunk(slot, c, top, total):
        for i in range(c * CHUNK, (c + 1) * CHUNK, SUBROWS):
            e = jnp.exp2(s_ref[slot, i : i + SUBROWS, :] - top)
            total = e if total is None else total + e
        return total

    def local_lse(half, row, top, total):
        lse_mine[half, pl.ds(row, 1), :] = top + jnp.log2(jnp.sum(total, axis=0, keepdims=True))

    def scores_of(slot):
        q2 = q_pair(slot)
        tops = None
        for c in range(NCHUNK):
            tops = score_chunk(slot, c, q2, tops)
        return jnp.max(tops, axis=0, keepdims=True)

    def turn(i):
        cols = pl.ds(pl.multiple_of(i * 2 * DIM, 2 * DIM), 2 * DIM)
        dt_ref[:, cols] = d_ref[cols, :].T

    def step_a(half):
        def body(i, tops):
            turn(i)
            new = []
            for k in range(2):
                slot = 2 * i + k
                q2 = q_pair(slot + 2)
                total = fresh = None
                for c in range(NCHUNK):
                    total = exp_chunk(slot, c, tops[k], total)
                    fresh = score_chunk(slot + 2, c, q2, fresh)
                local_lse(half, slot - 8 * half, tops[k], total)
                new.append(jnp.max(fresh, axis=0, keepdims=True))
            return tuple(new)

        return body

    def lse_copy(half, k):
        return pltpu.make_async_remote_copy(
            src_ref=lse_mine.at[half], dst_ref=lse_all.at[half, k - 1],
            send_sem=lse_ss.at[half, k - 1], recv_sem=lse_rs.at[half, k - 1],
            device_id=(qi, lax.rem(ti + k, 16)), device_id_type=MESH,
        )

    tops = lax.fori_loop(0, 4, step_a(0), (scores_of(0), scores_of(1)))
    pl.semaphore_wait(barrier, 19)
    for k in range(1, 16):
        lse_copy(0, k).start()
    tops = lax.fori_loop(4, 7, step_a(1), tops)
    turn(7)
    for k in range(2):
        total = None
        for c in range(NCHUNK):
            total = exp_chunk(14 + k, c, tops[k], total)
        local_lse(1, 6 + k, tops[k], total)
    for k in range(1, 16):
        lse_copy(1, k).start()

    lane_query = lax.broadcasted_iota(jnp.int32, (1, BLK), 1) // QLEN
    for slot in range(NBLK):
        half, y, cb = slot // 8, (slot % 8) // 2, slot % 2
        block = 4 * y + 2 * ((half + y) % 2) + cb
        w = jnp.zeros((1, BLK), F32)
        for g in range(BLK // QLEN):
            w = jnp.where(lane_query == g, cot_ref[block * (BLK // QLEN) + g], w)
        w_ref[slot : slot + 1, :] = w

    def doc_rows(x, zh):
        return pl.ds(pl.multiple_of((2 * x + zh) * BLK, BLK), BLK)

    def probs_of(slot, zh, acc):
        lse = lse_ref[pl.ds(slot, 1), :]
        w = w_ref[pl.ds(slot, 1), :]
        for x in range(4):
            rows = doc_rows(x, zh)
            p = jnp.exp2(s_ref[slot, rows, :] - lse)
            u_ref[slot, rows, :] = (w * p).astype(BF16)
            acc = acc + jnp.dot(dt_ref[:, rows], p.astype(BF16), preferred_element_type=F32)
        return acc

    def query_grads(slot):
        acc = probs_of(slot, zh0, acc_ref[slot])
        return (w_ref[pl.ds(slot, 1), :] * acc).T

    def pair_copy(st):
        return pltpu.make_async_remote_copy(
            src_ref=pair_out.at[st], dst_ref=pair_in.at[st],
            send_sem=pair_ss.at[st], recv_sem=pair_rs.at[st],
            device_id=(qi, ti + 1 - 2 * core), device_id_type=MESH,
        )

    def target(st):
        half, k = st // 4, lax.rem(st, 4)
        y = lax.rem(y0 + 1 + k, 4)
        return k, y, lax.rem(half + y, 2)

    def q_copy(st):
        k, y, z = target(st)
        slot = 2 * k + z0
        return pltpu.make_async_remote_copy(
            src_ref=q_out.at[st], dst_ref=q_in.at[slot],
            send_sem=q_ss.at[st], recv_sem=q_rs.at[slot],
            device_id=(qi, 4 * y + 2 * z + core), device_id_type=MESH,
        )

    def finish(st):
        pair_copy(st).wait_recv()
        both = part[st] + pair_in[st]
        part[st] = both
        q_out[st] = both.astype(BF16)

    def is_remote(st):
        k, y, z = target(st)
        return jnp.logical_or(k != 3, z != z0)

    def send(st):
        @pl.when(is_remote(st))
        def _():
            q_copy(st).start()

    def step_b(i, _):
        for st in (2 * i, 2 * i + 1):
            _, y, _ = target(st)
            base = 8 * (st // 4) + 2 * y
            pair_out[st] = query_grads(base + 1 - core)
            part[st] = query_grads(base + core)
        for st in (2 * i, 2 * i + 1):
            pair_copy(st).start()

        @pl.when(i > 0)
        def _():
            for st in (2 * i - 2, 2 * i - 1):
                finish(st)
            for st in (2 * i - 2, 2 * i - 1):
                send(st)

        return 0

    for half in range(2):
        for k in range(1, 16):
            lse_copy(half, k).wait_recv()
        top = lse_mine[half]
        for k in range(15):
            top = jnp.maximum(top, lse_all[half, k])
        total = jnp.exp2(lse_mine[half] - top)
        for k in range(15):
            total = total + jnp.exp2(lse_all[half, k] - top)
        lse_ref[8 * half : 8 * half + 8, :] = top + jnp.log2(total)
        for slot in range(8 * half, 8 * half + 8):
            acc_ref[slot] = probs_of(slot, 1 - zh0, jnp.zeros((DIM, BLK), F32))

    def d_target(m):
        m = lax.rem(m, 4)
        return lax.rem(x0 + jnp.where(m == 2, 3, jnp.where(m == 3, 0, 2 - m)), 4)

    def d_copy(m):
        device = 2 * x0 + 1 - zh0 if m is Z_COPY else 2 * d_target(m) + zh0
        m = 3 if m is Z_COPY else m
        return pltpu.make_async_remote_copy(
            src_ref=d_out.at[m], dst_ref=d_in.at[m],
            send_sem=d_ss.at[m], recv_sem=d_rs.at[m],
            device_id=(device, ti), device_id_type=MESH,
        )

    def docs_of(m, zh):
        rows = doc_rows(d_target(m), zh)
        acc = jnp.zeros((BLK, DIM), F32)
        for slot in range(NBLK):
            half, y, cb = slot // 8, (slot % 8) // 2, slot % 2
            blk = 4 * y + 2 * ((half + y) % 2) + cb
            acc = acc + jnp.dot(
                u_ref[slot, rows, :], q_ref[blk * BLK : (blk + 1) * BLK, :], preferred_element_type=F32
            )
        return acc

    def step_c(zh):
        def body(m, _):
            d_out[m] = docs_of(m, zh).astype(BF16)
            d_copy(m).start()
            return 0

        return body

    lax.fori_loop(0, 3, step_c(1 - zh0), 0)
    d_own[...] = docs_of(3, 1 - zh0)
    lax.fori_loop(0, 4, step_b, 0)
    for m in range(3):
        d_copy(m).wait_recv()
    total = d_own[...]
    for m in range(3):
        total = total + d_in[m].astype(F32)
    d_out[3] = total.astype(BF16)
    lax.fori_loop(4, 5, step_c(zh0), 0)
    d_copy(Z_COPY).start()
    for st in (6, 7):
        finish(st)
    for st in (6, 7):
        send(st)
    lax.fori_loop(5, 7, step_c(zh0), 0)
    d_own[...] = docs_of(7, zh0)

    mine = jnp.where(lax.rem(y0 + z0, 2) == 0, 3, 7)
    gq_ref[...] = part[mine]
    for k in range(4):
        for z in range(2):
            slot = 2 * k + z

            def add(slot=slot):
                q_copy_in = pltpu.make_async_remote_copy(
                    src_ref=q_out.at[0], dst_ref=q_in.at[slot],
                    send_sem=q_ss.at[0], recv_sem=q_rs.at[slot],
                    device_id=(qi, lax.rem(ti + 2, 16)), device_id_type=MESH,
                )
                q_copy_in.wait_recv()
                gq_ref[...] += q_in[slot].astype(F32)

            if k < 3:
                add()
            else:
                pl.when(z != z0)(add)
    total = d_own[...]
    for m in (Z_COPY, 4, 5, 6):
        d_copy(m).wait_recv()
        total = total + d_in[3 if m is Z_COPY else m].astype(F32)
    gd_ref[0] = total

    for half in range(2):
        for k in range(1, 16):
            lse_copy(half, k).wait_send()
    for st in range(8):
        pair_copy(st).wait_send()

        @pl.when(is_remote(st))
        def _():
            q_copy(st).wait_send()

    for m in (0, 1, 2, Z_COPY, 4, 5, 6):
        d_copy(m).wait_send()


def shards(queries, documents, cotangent):
    vmem = pl.BlockSpec(memory_space=pltpu.VMEM)
    dma = pltpu.SemaphoreType.DMA
    n_docs = documents.shape[0]
    return pl.pallas_call(
        kernel,
        out_shape=(
            jax.ShapeDtypeStruct((BLK, DIM), F32),
            jax.ShapeDtypeStruct((1, BLK, DIM), F32),
        ),
        in_specs=[vmem, vmem, pl.BlockSpec(memory_space=pltpu.SMEM)],
        out_specs=(vmem, vmem),
        scratch_shapes=[
            pltpu.VMEM((NBLK, n_docs, BLK), F32),
            pltpu.VMEM((NBLK, n_docs, BLK), BF16),
            pltpu.VMEM((n_docs, 2 * DIM), BF16),
            pltpu.VMEM((DIM, n_docs), BF16),
            pltpu.VMEM((NBLK, DIM, BLK), F32),
            pltpu.VMEM((NBLK, BLK), F32),
            pltpu.VMEM((2, 8, BLK), F32),
            pltpu.VMEM((2, 15, 8, BLK), F32),
            pltpu.VMEM((NBLK, BLK), F32),
            pltpu.VMEM((8, BLK, DIM), F32),
            pltpu.VMEM((8, BLK, DIM), F32),
            pltpu.VMEM((8, BLK, DIM), F32),
            pltpu.VMEM((8, BLK, DIM), BF16),
            pltpu.VMEM((8, BLK, DIM), BF16),
            pltpu.VMEM((7, BLK, DIM), BF16),
            pltpu.VMEM((7, BLK, DIM), BF16),
            pltpu.VMEM((BLK, DIM), F32),
            dma((2, 15)), dma((2, 15)), dma((8,)), dma((8,)),
            dma((8,)), dma((8,)), dma((7,)), dma((7,)),
        ],
        compiler_params=pltpu.CompilerParams(
            collective_id=0, has_side_effects=True, vmem_limit_bytes=67043328
        ),
    )(queries, documents, cotangent)


def solution(mesh):
    placed = (P("query", None), P("tok", None), P("query"))
    return jax.shard_map(
        shards,
        mesh=mesh,
        in_specs=placed,
        out_specs=(P(("query", "tok"), None), P("tok", "query", None)),
        check_vma=False,
    )
```

```python
import functools

import jax
import jax.numpy as jnp
from jax import lax
from jax.experimental import pallas as pl
from jax.experimental.pallas import tpu as pltpu
from jax.sharding import PartitionSpec as P

QLEN = 32
inv_temp = 2.0
LOG2E = 1.4426950408889634
SCALE = inv_temp * LOG2E

MESH = pl.DeviceIdType.MESH
F32 = jnp.float32
BF16 = jnp.bfloat16

BLK = 256
NBLK = 16
NDBLK = 8
DIM = 128
CHUNK = 256
NCHUNK = 8
SUBROWS = 16
Z_COPY = None
VMEM_LIMIT = 62 * 2**20


def block_of(slot):
    half, rest = slot // 8, lax.rem(slot, 8)
    y, core = rest // 2, lax.rem(rest, 2)
    return 4 * y + 2 * lax.rem(half + y, 2) + core


def kernel(
    q_ref, d_ref, cot_ref, gq_ref, gd_ref,
    s_ref, u_ref, dc_ref, dt_ref, w_ref, lse_mine, lse_all, lse_ref,
    pair_out, pair_in, part, q_out, q_in, d_out, d_in, d_own,
    lse_ss, lse_rs, pair_ss, pair_rs, q_ss, q_rs, d_ss, d_rs,
):
    qi, ti = lax.axis_index("query"), lax.axis_index("tok")
    x0, zh0 = qi // 2, lax.rem(qi, 2)
    y0, z0, core = ti // 4, lax.rem(ti // 2, 2), lax.rem(ti, 2)

    barrier = pltpu.get_barrier_semaphore()
    for k in range(1, 16):
        pl.semaphore_signal(barrier, inc=1, device_id=(qi, lax.rem(ti + k, 16)), device_id_type=MESH)
    for k in range(1, 4):
        pl.semaphore_signal(barrier, inc=1, device_id=(2 * lax.rem(x0 + k, 4) + zh0, ti), device_id_type=MESH)
    pl.semaphore_signal(barrier, inc=1, device_id=(2 * x0 + 1 - zh0, ti), device_id_type=MESH)

    for c in range(NCHUNK):
        rows = slice(c * CHUNK, (c + 1) * CHUNK)
        scaled = d_ref[rows, :].astype(F32) * SCALE
        high = scaled.astype(BF16)
        dc_ref[rows, 0:DIM] = high
        dc_ref[rows, DIM : 2 * DIM] = (scaled - high.astype(F32)).astype(BF16)

    def q_pair(slot):
        rows = q_ref[pl.ds(pl.multiple_of(block_of(slot) * BLK, BLK), BLK), :]
        return jnp.concatenate([rows, rows], axis=1)

    def score_chunk(slot, c, q2, tops):
        rows = slice(c * CHUNK, (c + 1) * CHUNK)
        s = lax.dot_general(dc_ref[rows, :], q2, (((1,), (1,)), ((), ())), preferred_element_type=F32)
        s_ref[slot, rows, :] = s
        for i in range(0, CHUNK, SUBROWS):
            part_s = s[i : i + SUBROWS]
            tops = part_s if tops is None else jnp.maximum(tops, part_s)
        return tops

    def exp_chunk(slot, c, top, total):
        for i in range(c * CHUNK, (c + 1) * CHUNK, SUBROWS):
            e = jnp.exp2(s_ref[slot, i : i + SUBROWS, :] - top)
            total = e if total is None else total + e
        return total

    def local_lse(half, row, top, total):
        lse_mine[half, pl.ds(row, 1), :] = top + jnp.log2(jnp.sum(total, axis=0, keepdims=True))

    def scores_of(slot):
        q2 = q_pair(slot)
        tops = None
        for c in range(NCHUNK):
            tops = score_chunk(slot, c, q2, tops)
        return jnp.max(tops, axis=0, keepdims=True)

    def turn(i):
        cols = pl.ds(pl.multiple_of(i * 2 * DIM, 2 * DIM), 2 * DIM)
        dt_ref[:, cols] = d_ref[cols, :].T

    def step_a(half):
        def body(i, tops):
            turn(i)
            new = []
            for k in range(2):
                slot = 2 * i + k
                q2 = q_pair(slot + 2)
                total = fresh = None
                for c in range(NCHUNK):
                    total = exp_chunk(slot, c, tops[k], total)
                    fresh = score_chunk(slot + 2, c, q2, fresh)
                local_lse(half, slot - 8 * half, tops[k], total)
                new.append(jnp.max(fresh, axis=0, keepdims=True))
            return tuple(new)

        return body

    def lse_copy(half, k):
        return pltpu.make_async_remote_copy(
            src_ref=lse_mine.at[half], dst_ref=lse_all.at[half, k - 1],
            send_sem=lse_ss.at[half, k - 1], recv_sem=lse_rs.at[half, k - 1],
            device_id=(qi, lax.rem(ti + k, 16)), device_id_type=MESH,
        )

    tops = lax.fori_loop(0, 4, step_a(0), (scores_of(0), scores_of(1)))
    pl.semaphore_wait(barrier, 19)
    for k in range(1, 16):
        lse_copy(0, k).start()
    tops = lax.fori_loop(4, 7, step_a(1), tops)
    turn(7)
    for k in range(2):
        total = None
        for c in range(NCHUNK):
            total = exp_chunk(14 + k, c, tops[k], total)
        local_lse(1, 6 + k, tops[k], total)
    for k in range(1, 16):
        lse_copy(1, k).start()

    lane_query = lax.broadcasted_iota(jnp.int32, (1, BLK), 1) // QLEN
    for slot in range(NBLK):
        half, y, cb = slot // 8, (slot % 8) // 2, slot % 2
        block = 4 * y + 2 * ((half + y) % 2) + cb
        w = jnp.zeros((1, BLK), F32)
        for g in range(BLK // QLEN):
            w = jnp.where(lane_query == g, cot_ref[block * (BLK // QLEN) + g], w)
        w_ref[slot : slot + 1, :] = w

    def doc_rows(x, zh):
        return pl.ds(pl.multiple_of((2 * x + zh) * BLK, BLK), BLK)

    def query_grads(slot):
        lse = lse_ref[pl.ds(slot, 1), :]
        w = w_ref[pl.ds(slot, 1), :]
        acc = jnp.zeros((DIM, BLK), F32)
        for c in range(NCHUNK):
            rows = slice(c * CHUNK, (c + 1) * CHUNK)
            p = jnp.exp2(s_ref[slot, rows, :] - lse)
            u_ref[slot, rows, :] = (w * p).astype(BF16)
            acc = acc + jnp.dot(dt_ref[:, rows], p.astype(BF16), preferred_element_type=F32)
        return (w * acc).T

    def pair_copy(st):
        return pltpu.make_async_remote_copy(
            src_ref=pair_out.at[st], dst_ref=pair_in.at[st],
            send_sem=pair_ss.at[st], recv_sem=pair_rs.at[st],
            device_id=(qi, ti + 1 - 2 * core), device_id_type=MESH,
        )

    def target(st):
        half, k = st // 4, lax.rem(st, 4)
        y = lax.rem(y0 + 1 + k, 4)
        return k, y, lax.rem(half + y, 2)

    def q_copy(st):
        k, y, z = target(st)
        slot = 2 * k + z0
        return pltpu.make_async_remote_copy(
            src_ref=q_out.at[st], dst_ref=q_in.at[slot],
            send_sem=q_ss.at[st], recv_sem=q_rs.at[slot],
            device_id=(qi, 4 * y + 2 * z + core), device_id_type=MESH,
        )

    def finish(st):
        pair_copy(st).wait_recv()
        both = part[st] + pair_in[st]
        part[st] = both
        q_out[st] = both.astype(BF16)

    def is_remote(st):
        k, y, z = target(st)
        return jnp.logical_or(k != 3, z != z0)

    def send(st):
        @pl.when(is_remote(st))
        def _():
            q_copy(st).start()

    def step_b(i, _):
        for st in (2 * i, 2 * i + 1):
            _, y, _ = target(st)
            base = 8 * (st // 4) + 2 * y
            pair_out[st] = query_grads(base + 1 - core)
            part[st] = query_grads(base + core)
        for st in (2 * i, 2 * i + 1):
            pair_copy(st).start()

        @pl.when(i > 0)
        def _():
            for st in (2 * i - 2, 2 * i - 1):
                finish(st)
            for st in (2 * i - 2, 2 * i - 1):
                send(st)

        return 0

    for half in range(2):
        for k in range(1, 16):
            lse_copy(half, k).wait_recv()
        top = lse_mine[half]
        for k in range(15):
            top = jnp.maximum(top, lse_all[half, k])
        total = jnp.exp2(lse_mine[half] - top)
        for k in range(15):
            total = total + jnp.exp2(lse_all[half, k] - top)
        lse_ref[8 * half : 8 * half + 8, :] = top + jnp.log2(total)
        lax.fori_loop(2 * half, 2 * half + 2, step_b, 0)

    def d_target(m):
        m = lax.rem(m, 4)
        return lax.rem(x0 + jnp.where(m == 2, 3, jnp.where(m == 3, 0, 2 - m)), 4)

    def d_copy(m):
        device = 2 * x0 + 1 - zh0 if m is Z_COPY else 2 * d_target(m) + zh0
        m = 3 if m is Z_COPY else m
        return pltpu.make_async_remote_copy(
            src_ref=d_out.at[m], dst_ref=d_in.at[m],
            send_sem=d_ss.at[m], recv_sem=d_rs.at[m],
            device_id=(device, ti), device_id_type=MESH,
        )

    def docs_of(m, zh):
        rows = doc_rows(d_target(m), zh)
        acc = jnp.zeros((BLK, DIM), F32)
        for slot in range(NBLK):
            half, y, cb = slot // 8, (slot % 8) // 2, slot % 2
            blk = 4 * y + 2 * ((half + y) % 2) + cb
            acc = acc + jnp.dot(
                u_ref[slot, rows, :], q_ref[blk * BLK : (blk + 1) * BLK, :], preferred_element_type=F32
            )
        return acc

    def step_c(zh):
        def body(m, _):
            d_out[m] = docs_of(m, zh).astype(BF16)
            d_copy(m).start()
            return 0

        return body

    lax.fori_loop(0, 1, step_c(1 - zh0), 0)
    for st in (6, 7):
        finish(st)
    for st in (6, 7):
        send(st)
    lax.fori_loop(1, 3, step_c(1 - zh0), 0)
    d_own[...] = docs_of(3, 1 - zh0)
    lax.fori_loop(4, 7, step_c(zh0), 0)
    total = d_own[...]
    for m in range(3):
        d_copy(m).wait_recv()
        total = total + d_in[m].astype(F32)
    d_out[3] = total.astype(BF16)
    d_copy(Z_COPY).start()
    d_own[...] = docs_of(7, zh0)

    mine = jnp.where(lax.rem(y0 + z0, 2) == 0, 3, 7)
    gq_ref[...] = part[mine]
    for k in range(4):
        for z in range(2):
            slot = 2 * k + z

            def add(slot=slot):
                q_copy_in = pltpu.make_async_remote_copy(
                    src_ref=q_out.at[0], dst_ref=q_in.at[slot],
                    send_sem=q_ss.at[0], recv_sem=q_rs.at[slot],
                    device_id=(qi, lax.rem(ti + 2, 16)), device_id_type=MESH,
                )
                q_copy_in.wait_recv()
                gq_ref[...] += q_in[slot].astype(F32)

            if k < 3:
                add()
            else:
                pl.when(z != z0)(add)
    total = d_own[...]
    for m in (Z_COPY, 4, 5, 6):
        d_copy(m).wait_recv()
        total = total + d_in[3 if m is Z_COPY else m].astype(F32)
    gd_ref[0] = total

    for half in range(2):
        for k in range(1, 16):
            lse_copy(half, k).wait_send()
    for st in range(8):
        pair_copy(st).wait_send()

        @pl.when(is_remote(st))
        def _():
            q_copy(st).wait_send()

    for m in (0, 1, 2, Z_COPY, 4, 5, 6):
        d_copy(m).wait_send()


def put_out(gq_in, gd_in, gq_out, gd_out, sems):
    copies = [pltpu.make_async_copy(gq_in, gq_out, sems.at[0]), pltpu.make_async_copy(gd_in, gd_out, sems.at[1])]
    for copy in copies:
        copy.start()
    for copy in copies:
        copy.wait()


def shards(queries, documents, cotangent):
    vmem = pl.BlockSpec(memory_space=pltpu.VMEM)
    dma = pltpu.SemaphoreType.DMA
    n_docs = documents.shape[0]
    grads = pl.pallas_call(
        kernel,
        out_shape=(
            pltpu.VMEM((BLK, DIM), F32),
            pltpu.VMEM((1, BLK, DIM), F32),
        ),
        in_specs=[vmem, vmem, pl.BlockSpec(memory_space=pltpu.SMEM)],
        out_specs=(vmem, vmem),
        scratch_shapes=[
            pltpu.VMEM((NBLK, n_docs, BLK), F32),
            pltpu.VMEM((NBLK, n_docs, BLK), BF16),
            pltpu.VMEM((n_docs, 2 * DIM), BF16),
            pltpu.VMEM((DIM, n_docs), BF16),
            pltpu.VMEM((NBLK, BLK), F32),
            pltpu.VMEM((2, 8, BLK), F32),
            pltpu.VMEM((2, 15, 8, BLK), F32),
            pltpu.VMEM((NBLK, BLK), F32),
            pltpu.VMEM((8, BLK, DIM), F32),
            pltpu.VMEM((8, BLK, DIM), F32),
            pltpu.VMEM((8, BLK, DIM), F32),
            pltpu.VMEM((8, BLK, DIM), BF16),
            pltpu.VMEM((8, BLK, DIM), BF16),
            pltpu.VMEM((7, BLK, DIM), BF16),
            pltpu.VMEM((7, BLK, DIM), BF16),
            pltpu.VMEM((BLK, DIM), F32),
            dma((2, 15)), dma((2, 15)), dma((8,)), dma((8,)),
            dma((8,)), dma((8,)), dma((7,)), dma((7,)),
        ],
        compiler_params=pltpu.CompilerParams(
            collective_id=0, has_side_effects=True, vmem_limit_bytes=VMEM_LIMIT
        ),
    )(queries, documents, cotangent)
    anywhere = pl.BlockSpec(memory_space=pl.ANY)
    return pl.pallas_call(
        put_out,
        out_shape=(
            jax.ShapeDtypeStruct((BLK, DIM), F32),
            jax.ShapeDtypeStruct((1, BLK, DIM), F32),
        ),
        in_specs=[vmem, vmem],
        out_specs=(anywhere, anywhere),
        scratch_shapes=[dma((2,))],
    )(*(pltpu.with_memory_space_constraint(g, pltpu.VMEM) for g in grads))


def solution(mesh):
    placed = (P("query", None), P("tok", None), P("query"))
    return jax.shard_map(
        shards,
        mesh=mesh,
        in_specs=placed,
        out_specs=(P(("query", "tok"), None), P("tok", "query", None)),
        check_vma=False,
    )
```

```python
import functools

import jax
import jax.numpy as jnp
from jax import lax
from jax.experimental import pallas as pl
from jax.experimental.pallas import tpu as pltpu
from jax.sharding import PartitionSpec as P

QLEN = 32
inv_temp = 2.0
LOG2E = 1.4426950408889634
SCALE = inv_temp * LOG2E

MESH = pl.DeviceIdType.MESH
F32 = jnp.float32
BF16 = jnp.bfloat16

BLK = 256
NBLK = 16
NDBLK = 8
DIM = 128
CHUNK = 256
NCHUNK = 8
SUBROWS = 16
Z_COPY = None
GROUPS = ((0, slice(0, 8)), (1, slice(0, 4)), (1, slice(4, 8)))
VMEM_LIMIT = 62 * 2**20


def block_of(slot):
    half, rest = slot // 8, lax.rem(slot, 8)
    y, core = rest // 2, lax.rem(rest, 2)
    return 4 * y + 2 * lax.rem(half + y, 2) + core


def kernel(
    q_in_hbm, d_in_hbm, cot_ref, gq_ref, gd_ref,
    q_ref, d_ref, in_sems,
    s_ref, u_ref, dc_ref, dt_ref, w_ref, lse_mine, lse_all, lse_ref,
    pair_out, pair_in, part, q_out, q_in, d_out, d_in, d_own,
    lse_ss, lse_rs, pair_ss, pair_rs, q_ss, q_rs, d_ss, d_rs,
):
    qi, ti = lax.axis_index("query"), lax.axis_index("tok")
    x0, zh0 = qi // 2, lax.rem(qi, 2)
    y0, z0, core = ti // 4, lax.rem(ti // 2, 2), lax.rem(ti, 2)

    fetch_d = pltpu.make_async_copy(d_in_hbm, d_ref, in_sems.at[0])
    fetch_q = pltpu.make_async_copy(q_in_hbm, q_ref, in_sems.at[1])
    fetch_d.start()
    fetch_q.start()
    barrier = pltpu.get_barrier_semaphore()
    for k in range(1, 16):
        pl.semaphore_signal(barrier, inc=1, device_id=(qi, lax.rem(ti + k, 16)), device_id_type=MESH)
    for k in range(1, 4):
        pl.semaphore_signal(barrier, inc=1, device_id=(2 * lax.rem(x0 + k, 4) + zh0, ti), device_id_type=MESH)
    pl.semaphore_signal(barrier, inc=1, device_id=(2 * x0 + 1 - zh0, ti), device_id_type=MESH)

    fetch_d.wait()
    for c in range(NCHUNK):
        rows = slice(c * CHUNK, (c + 1) * CHUNK)
        scaled = d_ref[rows, :].astype(F32) * SCALE
        high = scaled.astype(BF16)
        dc_ref[rows, 0:DIM] = high
        dc_ref[rows, DIM : 2 * DIM] = (scaled - high.astype(F32)).astype(BF16)

    fetch_q.wait()

    def q_pair(slot):
        rows = q_ref[pl.ds(pl.multiple_of(block_of(slot) * BLK, BLK), BLK), :]
        return jnp.concatenate([rows, rows], axis=1)

    def score_chunk(slot, c, q2, tops):
        rows = slice(c * CHUNK, (c + 1) * CHUNK)
        s = lax.dot_general(dc_ref[rows, :], q2, (((1,), (1,)), ((), ())), preferred_element_type=F32)
        s_ref[slot, rows, :] = s
        for i in range(0, CHUNK, SUBROWS):
            part_s = s[i : i + SUBROWS]
            tops = part_s if tops is None else jnp.maximum(tops, part_s)
        return tops

    def exp_chunk(slot, c, top, total):
        for i in range(c * CHUNK, (c + 1) * CHUNK, SUBROWS):
            e = jnp.exp2(s_ref[slot, i : i + SUBROWS, :] - top)
            total = e if total is None else total + e
        return total

    def local_lse(half, row, top, total):
        lse_mine[half, pl.ds(row, 1), :] = top + jnp.log2(jnp.sum(total, axis=0, keepdims=True))

    def scores_of(slot):
        q2 = q_pair(slot)
        tops = None
        for c in range(NCHUNK):
            tops = score_chunk(slot, c, q2, tops)
        return jnp.max(tops, axis=0, keepdims=True)

    def turn(i):
        cols = pl.ds(pl.multiple_of(i * 2 * DIM, 2 * DIM), 2 * DIM)
        dt_ref[:, cols] = d_ref[cols, :].T

    def step_a(half):
        def body(i, tops):
            turn(i)
            new = []
            for k in range(2):
                slot = 2 * i + k
                q2 = q_pair(slot + 2)
                total = fresh = None
                for c in range(NCHUNK):
                    total = exp_chunk(slot, c, tops[k], total)
                    fresh = score_chunk(slot + 2, c, q2, fresh)
                local_lse(half, slot - 8 * half, tops[k], total)
                new.append(jnp.max(fresh, axis=0, keepdims=True))
            return tuple(new)

        return body

    def lse_copy(group, k):
        half, rows = GROUPS[group]
        return pltpu.make_async_remote_copy(
            src_ref=lse_mine.at[half, rows], dst_ref=lse_all.at[half, k - 1, rows],
            send_sem=lse_ss.at[group, k - 1], recv_sem=lse_rs.at[group, k - 1],
            device_id=(qi, lax.rem(ti + k, 16)), device_id_type=MESH,
        )

    tops = lax.fori_loop(0, 4, step_a(0), (scores_of(0), scores_of(1)))
    pl.semaphore_wait(barrier, 19)
    for k in range(1, 16):
        lse_copy(0, k).start()
    tops = lax.fori_loop(4, 6, step_a(1), tops)
    for k in range(1, 16):
        lse_copy(1, k).start()
    tops = lax.fori_loop(6, 7, step_a(1), tops)
    turn(7)
    for k in range(2):
        total = None
        for c in range(NCHUNK):
            total = exp_chunk(14 + k, c, tops[k], total)
        local_lse(1, 6 + k, tops[k], total)
    for k in range(1, 16):
        lse_copy(2, k).start()

    lane_query = lax.broadcasted_iota(jnp.int32, (1, BLK), 1) // QLEN
    for slot in range(NBLK):
        half, y, cb = slot // 8, (slot % 8) // 2, slot % 2
        block = 4 * y + 2 * ((half + y) % 2) + cb
        w = jnp.zeros((1, BLK), F32)
        for g in range(BLK // QLEN):
            w = jnp.where(lane_query == g, cot_ref[block * (BLK // QLEN) + g], w)
        w_ref[slot : slot + 1, :] = w

    def doc_rows(x, zh):
        return pl.ds(pl.multiple_of((2 * x + zh) * BLK, BLK), BLK)

    def query_grads(slot):
        lse = lse_ref[pl.ds(slot, 1), :]
        w = w_ref[pl.ds(slot, 1), :]
        acc = jnp.zeros((DIM, BLK), F32)
        for c in range(NCHUNK):
            rows = slice(c * CHUNK, (c + 1) * CHUNK)
            p = jnp.exp2(s_ref[slot, rows, :] - lse)
            u_ref[slot, rows, :] = (w * p).astype(BF16)
            acc = acc + jnp.dot(dt_ref[:, rows], p.astype(BF16), preferred_element_type=F32)
        return (w * acc).T

    def pair_copy(st):
        return pltpu.make_async_remote_copy(
            src_ref=pair_out.at[st], dst_ref=pair_in.at[st],
            send_sem=pair_ss.at[st], recv_sem=pair_rs.at[st],
            device_id=(qi, ti + 1 - 2 * core), device_id_type=MESH,
        )

    def target(st):
        half, k = st // 4, lax.rem(st, 4)
        y = 2 * (k // 2) + lax.rem(y0 + 1 + k, 2)
        return y, lax.rem(half + y, 2)

    def q_copy(st):
        y, z = target(st)
        slot = 2 * y0 + z0
        return pltpu.make_async_remote_copy(
            src_ref=q_out.at[st], dst_ref=q_in.at[slot],
            send_sem=q_ss.at[st], recv_sem=q_rs.at[slot],
            device_id=(qi, 4 * y + 2 * z + core), device_id_type=MESH,
        )

    def finish(st):
        pair_copy(st).wait_recv()
        both = part[st] + pair_in[st]
        part[st] = both
        q_out[st] = both.astype(BF16)

    def is_remote(st):
        y, z = target(st)
        return 2 * y + z != 2 * y0 + z0

    def send(st):
        @pl.when(is_remote(st))
        def _():
            q_copy(st).start()

    def step_b(i, _):
        for st in (2 * i, 2 * i + 1):
            y, _ = target(st)
            base = 8 * (st // 4) + 2 * y
            pair_out[st] = query_grads(base + 1 - core)
            part[st] = query_grads(base + core)
        for st in (2 * i, 2 * i + 1):
            pair_copy(st).start()

        @pl.when(i > 0)
        def _():
            for st in (2 * i - 2, 2 * i - 1):
                finish(st)
            for st in (2 * i - 2, 2 * i - 1):
                send(st)

        return 0

    for group, (half, rows) in enumerate(GROUPS):
        for k in range(1, 16):
            lse_copy(group, k).wait_recv()
        top = lse_mine[half, rows]
        for k in range(15):
            top = jnp.maximum(top, lse_all[half, k, rows])
        total = jnp.exp2(lse_mine[half, rows] - top)
        for k in range(15):
            total = total + jnp.exp2(lse_all[half, k, rows] - top)
        lse_ref[8 * half + rows.start : 8 * half + rows.stop, :] = top + jnp.log2(total)
        lax.fori_loop(group + 1 if group else 0, group + 2, step_b, 0)

    def d_target(m):
        m = lax.rem(m, 4)
        return lax.rem(x0 + jnp.where(m == 2, 3, jnp.where(m == 3, 0, 2 - m)), 4)

    def d_copy(m):
        device = 2 * x0 + 1 - zh0 if m is Z_COPY else 2 * d_target(m) + zh0
        m = 3 if m is Z_COPY else m
        return pltpu.make_async_remote_copy(
            src_ref=d_out.at[m], dst_ref=d_in.at[m],
            send_sem=d_ss.at[m], recv_sem=d_rs.at[m],
            device_id=(device, ti), device_id_type=MESH,
        )

    def docs_of(m, zh):
        rows = doc_rows(d_target(m), zh)
        acc = jnp.zeros((BLK, DIM), F32)
        for slot in range(NBLK):
            half, y, cb = slot // 8, (slot % 8) // 2, slot % 2
            blk = 4 * y + 2 * ((half + y) % 2) + cb
            acc = acc + jnp.dot(
                u_ref[slot, rows, :], q_ref[blk * BLK : (blk + 1) * BLK, :], preferred_element_type=F32
            )
        return acc

    def step_c(zh):
        def body(m, _):
            d_out[m] = docs_of(m, zh).astype(BF16)
            d_copy(m).start()
            return 0

        return body

    lax.fori_loop(0, 1, step_c(1 - zh0), 0)
    for st in (6, 7):
        finish(st)
    for st in (6, 7):
        send(st)
    lax.fori_loop(1, 3, step_c(1 - zh0), 0)
    d_own[...] = docs_of(3, 1 - zh0)
    lax.fori_loop(4, 7, step_c(zh0), 0)
    total = d_own[...]
    for m in range(3):
        d_copy(m).wait_recv()
        total = total + d_in[m].astype(F32)
    d_out[3] = total.astype(BF16)
    d_copy(Z_COPY).start()
    d_own[...] = docs_of(7, zh0)

    gq_ref[...] = part[4 * lax.rem(y0 + z0, 2) + 2 * (y0 // 2) + 1]
    for slot in range(8):

        @pl.when(slot != 2 * y0 + z0)
        def _():
            pltpu.make_async_remote_copy(
                src_ref=q_out.at[0], dst_ref=q_in.at[slot],
                send_sem=q_ss.at[0], recv_sem=q_rs.at[slot],
                device_id=(qi, lax.rem(ti + 2, 16)), device_id_type=MESH,
            ).wait_recv()
            gq_ref[...] += q_in[slot].astype(F32)

    total = d_own[...]
    for m in (Z_COPY, 4, 5, 6):
        d_copy(m).wait_recv()
        total = total + d_in[3 if m is Z_COPY else m].astype(F32)
    gd_ref[0] = total

    for group in range(3):
        for k in range(1, 16):
            lse_copy(group, k).wait_send()
    for st in range(8):
        pair_copy(st).wait_send()

        @pl.when(is_remote(st))
        def _():
            q_copy(st).wait_send()

    for m in (0, 1, 2, Z_COPY, 4, 5, 6):
        d_copy(m).wait_send()


def put_out(gq_in, gd_in, gq_out, gd_out, sems):
    copies = [pltpu.make_async_copy(gq_in, gq_out, sems.at[0]), pltpu.make_async_copy(gd_in, gd_out, sems.at[1])]
    for copy in copies:
        copy.start()
    for copy in copies:
        copy.wait()


def shards(queries, documents, cotangent):
    vmem = pl.BlockSpec(memory_space=pltpu.VMEM)
    anywhere = pl.BlockSpec(memory_space=pl.ANY)
    dma = pltpu.SemaphoreType.DMA
    n_docs = documents.shape[0]
    grads = pl.pallas_call(
        kernel,
        out_shape=(
            pltpu.VMEM((BLK, DIM), F32),
            pltpu.VMEM((1, BLK, DIM), F32),
        ),
        in_specs=[anywhere, anywhere, pl.BlockSpec(memory_space=pltpu.SMEM)],
        out_specs=(vmem, vmem),
        scratch_shapes=[
            pltpu.VMEM(queries.shape, BF16),
            pltpu.VMEM(documents.shape, BF16),
            dma((2,)),
            pltpu.VMEM((NBLK, n_docs, BLK), F32),
            pltpu.VMEM((NBLK, n_docs, BLK), BF16),
            pltpu.VMEM((n_docs, 2 * DIM), BF16),
            pltpu.VMEM((DIM, n_docs), BF16),
            pltpu.VMEM((NBLK, BLK), F32),
            pltpu.VMEM((2, 8, BLK), F32),
            pltpu.VMEM((2, 15, 8, BLK), F32),
            pltpu.VMEM((NBLK, BLK), F32),
            pltpu.VMEM((8, BLK, DIM), F32),
            pltpu.VMEM((8, BLK, DIM), F32),
            pltpu.VMEM((8, BLK, DIM), F32),
            pltpu.VMEM((8, BLK, DIM), BF16),
            pltpu.VMEM((8, BLK, DIM), BF16),
            pltpu.VMEM((7, BLK, DIM), BF16),
            pltpu.VMEM((7, BLK, DIM), BF16),
            pltpu.VMEM((BLK, DIM), F32),
            dma((3, 15)), dma((3, 15)), dma((8,)), dma((8,)),
            dma((8,)), dma((8,)), dma((7,)), dma((7,)),
        ],
        compiler_params=pltpu.CompilerParams(
            collective_id=0, has_side_effects=True, vmem_limit_bytes=VMEM_LIMIT
        ),
    )(queries, documents, cotangent)
    return pl.pallas_call(
        put_out,
        out_shape=(
            jax.ShapeDtypeStruct((BLK, DIM), F32),
            jax.ShapeDtypeStruct((1, BLK, DIM), F32),
        ),
        in_specs=[vmem, vmem],
        out_specs=(anywhere, anywhere),
        scratch_shapes=[dma((2,))],
    )(*(pltpu.with_memory_space_constraint(g, pltpu.VMEM) for g in grads))


def solution(mesh):
    placed = (P("query", None), P("tok", None), P("query"))
    return jax.shard_map(
        shards,
        mesh=mesh,
        in_specs=placed,
        out_specs=(P(("query", "tok"), None), P("tok", "query", None)),
        check_vma=False,
    )
```

```python
import functools

import jax
import jax.numpy as jnp
from jax import lax
from jax.experimental import pallas as pl
from jax.experimental.pallas import tpu as pltpu
from jax.sharding import PartitionSpec as P

QLEN = 32
inv_temp = 2.0
LOG2E = 1.4426950408889634
SCALE = inv_temp * LOG2E

MESH = pl.DeviceIdType.MESH
F32 = jnp.float32
BF16 = jnp.bfloat16

BLK = 256
NBLK = 16
NDBLK = 8
DIM = 128
CHUNK = 256
NCHUNK = 8
SUBROWS = 16
Z_COPY = None
VMEM_LIMIT = 62 * 2**20


def block_of(slot):
    half, rest = slot // 8, lax.rem(slot, 8)
    y, core = rest // 2, lax.rem(rest, 2)
    return 4 * y + 2 * lax.rem(half + y, 2) + core


def kernel(
    q_in_hbm, d_in_hbm, cot_ref, gq_ref, gd_ref,
    q_ref, d_ref, in_sems,
    s_ref, u_ref, dc_ref, dt_ref, w_ref, lse_mine, lse_all, lse_ref,
    pair_out, pair_in, part, q_out, q_in, d_out, d_in, d_own,
    lse_ss, lse_rs, pair_ss, pair_rs, q_ss, q_rs, d_ss, d_rs,
):
    qi, ti = lax.axis_index("query"), lax.axis_index("tok")
    x0, zh0 = qi // 2, lax.rem(qi, 2)
    y0, z0, core = ti // 4, lax.rem(ti // 2, 2), lax.rem(ti, 2)

    fetch_d = pltpu.make_async_copy(d_in_hbm, d_ref, in_sems.at[0])
    fetch_q = pltpu.make_async_copy(q_in_hbm, q_ref, in_sems.at[1])
    fetch_d.start()
    fetch_q.start()
    barrier = pltpu.get_barrier_semaphore()
    for k in range(1, 16):
        pl.semaphore_signal(barrier, inc=1, device_id=(qi, lax.rem(ti + k, 16)), device_id_type=MESH)
    for k in range(1, 4):
        pl.semaphore_signal(barrier, inc=1, device_id=(2 * lax.rem(x0 + k, 4) + zh0, ti), device_id_type=MESH)
    pl.semaphore_signal(barrier, inc=1, device_id=(2 * x0 + 1 - zh0, ti), device_id_type=MESH)

    fetch_d.wait()
    for c in range(NCHUNK):
        rows = slice(c * CHUNK, (c + 1) * CHUNK)
        scaled = d_ref[rows, :].astype(F32) * SCALE
        high = scaled.astype(BF16)
        dc_ref[rows, 0:DIM] = high
        dc_ref[rows, DIM : 2 * DIM] = (scaled - high.astype(F32)).astype(BF16)

    fetch_q.wait()

    def q_pair(slot):
        rows = q_ref[pl.ds(pl.multiple_of(block_of(slot) * BLK, BLK), BLK), :]
        return jnp.concatenate([rows, rows], axis=1)

    def score_chunk(slot, c, q2, tops):
        rows = slice(c * CHUNK, (c + 1) * CHUNK)
        s = lax.dot_general(dc_ref[rows, :], q2, (((1,), (1,)), ((), ())), preferred_element_type=F32)
        s_ref[slot, rows, :] = s
        for i in range(0, CHUNK, SUBROWS):
            part_s = s[i : i + SUBROWS]
            tops = part_s if tops is None else jnp.maximum(tops, part_s)
        return tops

    def exp_chunk(slot, c, top, total):
        for i in range(c * CHUNK, (c + 1) * CHUNK, SUBROWS):
            e = jnp.exp2(s_ref[slot, i : i + SUBROWS, :] - top)
            total = e if total is None else total + e
        return total

    def local_lse(half, row, top, total):
        lse_mine[half, pl.ds(row, 1), :] = top + jnp.log2(jnp.sum(total, axis=0, keepdims=True))

    def scores_of(slot):
        q2 = q_pair(slot)
        tops = None
        for c in range(NCHUNK):
            tops = score_chunk(slot, c, q2, tops)
        return jnp.max(tops, axis=0, keepdims=True)

    def turn(i):
        cols = pl.ds(pl.multiple_of(i * 2 * DIM, 2 * DIM), 2 * DIM)
        dt_ref[:, cols] = d_ref[cols, :].T

    def step_a(half):
        def body(i, tops):
            turn(i)
            new = []
            for k in range(2):
                slot = 2 * i + k
                q2 = q_pair(slot + 2)
                total = fresh = None
                for c in range(NCHUNK):
                    total = exp_chunk(slot, c, tops[k], total)
                    fresh = score_chunk(slot + 2, c, q2, fresh)
                local_lse(half, slot - 8 * half, tops[k], total)
                new.append(jnp.max(fresh, axis=0, keepdims=True))
            return tuple(new)

        return body

    def lse_copy(half, k):
        return pltpu.make_async_remote_copy(
            src_ref=lse_mine.at[half], dst_ref=lse_all.at[half, k - 1],
            send_sem=lse_ss.at[half, k - 1], recv_sem=lse_rs.at[half, k - 1],
            device_id=(qi, lax.rem(ti + k, 16)), device_id_type=MESH,
        )

    tops = lax.fori_loop(0, 4, step_a(0), (scores_of(0), scores_of(1)))
    pl.semaphore_wait(barrier, 19)
    for k in range(1, 16):
        lse_copy(0, k).start()
    tops = lax.fori_loop(4, 7, step_a(1), tops)
    turn(7)
    for k in range(2):
        total = None
        for c in range(NCHUNK):
            total = exp_chunk(14 + k, c, tops[k], total)
        local_lse(1, 6 + k, tops[k], total)
    for k in range(1, 16):
        lse_copy(1, k).start()

    lane_query = lax.broadcasted_iota(jnp.int32, (1, BLK), 1) // QLEN
    for slot in range(NBLK):
        half, y, cb = slot // 8, (slot % 8) // 2, slot % 2
        block = 4 * y + 2 * ((half + y) % 2) + cb
        w = jnp.zeros((1, BLK), F32)
        for g in range(BLK // QLEN):
            w = jnp.where(lane_query == g, cot_ref[block * (BLK // QLEN) + g], w)
        w_ref[slot : slot + 1, :] = w

    def doc_rows(x, zh):
        return pl.ds(pl.multiple_of((2 * x + zh) * BLK, BLK), BLK)

    def query_grads(slot):
        lse = lse_ref[pl.ds(slot, 1), :]
        w = w_ref[pl.ds(slot, 1), :]
        acc = jnp.zeros((DIM, BLK), F32)
        for c in range(NCHUNK):
            rows = slice(c * CHUNK, (c + 1) * CHUNK)
            p = jnp.exp2(s_ref[slot, rows, :] - lse)
            u_ref[slot, rows, :] = (w * p).astype(BF16)
            acc = acc + jnp.dot(dt_ref[:, rows], p.astype(BF16), preferred_element_type=F32)
        return (w * acc).T

    def pair_copy(st):
        return pltpu.make_async_remote_copy(
            src_ref=pair_out.at[st], dst_ref=pair_in.at[st],
            send_sem=pair_ss.at[st], recv_sem=pair_rs.at[st],
            device_id=(qi, ti + 1 - 2 * core), device_id_type=MESH,
        )

    def target(st):
        half, k = st // 4, lax.rem(st, 4)
        y = lax.rem(y0 + 1 + k, 4)
        return k, y, lax.rem(half + y, 2)

    def q_copy(st):
        k, y, z = target(st)
        slot = 2 * k + z0
        return pltpu.make_async_remote_copy(
            src_ref=q_out.at[st], dst_ref=q_in.at[slot],
            send_sem=q_ss.at[st], recv_sem=q_rs.at[slot],
            device_id=(qi, 4 * y + 2 * z + core), device_id_type=MESH,
        )

    def finish(st):
        pair_copy(st).wait_recv()
        both = part[st] + pair_in[st]
        part[st] = both
        q_out[st] = both.astype(BF16)

    def is_remote(st):
        k, y, z = target(st)
        return jnp.logical_or(k != 3, z != z0)

    def send(st):
        @pl.when(is_remote(st))
        def _():
            q_copy(st).start()

    def step_b(i, _):
        for st in (2 * i, 2 * i + 1):
            _, y, _ = target(st)
            base = 8 * (st // 4) + 2 * y
            pair_out[st] = query_grads(base + 1 - core)
            part[st] = query_grads(base + core)
        for st in (2 * i, 2 * i + 1):
            pair_copy(st).start()

        @pl.when(i > 0)
        def _():
            for st in (2 * i - 2, 2 * i - 1):
                finish(st)
            for st in (2 * i - 2, 2 * i - 1):
                send(st)

        return 0

    for half in range(2):
        for k in range(1, 16):
            lse_copy(half, k).wait_recv()
        top = lse_mine[half]
        for k in range(15):
            top = jnp.maximum(top, lse_all[half, k])
        total = jnp.exp2(lse_mine[half] - top)
        for k in range(15):
            total = total + jnp.exp2(lse_all[half, k] - top)
        lse_ref[8 * half : 8 * half + 8, :] = top + jnp.log2(total)
        lax.fori_loop(2 * half, 2 * half + 2, step_b, 0)

    def d_target(m):
        m = lax.rem(m, 4)
        return lax.rem(x0 + jnp.where(m == 2, 3, jnp.where(m == 3, 0, 2 - m)), 4)

    def d_copy(m):
        device = 2 * x0 + 1 - zh0 if m is Z_COPY else 2 * d_target(m) + zh0
        m = 3 if m is Z_COPY else m
        return pltpu.make_async_remote_copy(
            src_ref=d_out.at[m], dst_ref=d_in.at[m],
            send_sem=d_ss.at[m], recv_sem=d_rs.at[m],
            device_id=(device, ti), device_id_type=MESH,
        )

    def docs_of(m, zh):
        rows = doc_rows(d_target(m), zh)
        acc = jnp.zeros((BLK, DIM), F32)
        for slot in range(NBLK):
            half, y, cb = slot // 8, (slot % 8) // 2, slot % 2
            blk = 4 * y + 2 * ((half + y) % 2) + cb
            acc = acc + jnp.dot(
                u_ref[slot, rows, :], q_ref[blk * BLK : (blk + 1) * BLK, :], preferred_element_type=F32
            )
        return acc

    def step_c(zh):
        def body(m, _):
            d_out[m] = docs_of(m, zh).astype(BF16)
            d_copy(m).start()
            return 0

        return body

    lax.fori_loop(0, 1, step_c(1 - zh0), 0)
    for st in (6, 7):
        finish(st)
    for st in (6, 7):
        send(st)
    lax.fori_loop(1, 3, step_c(1 - zh0), 0)
    d_own[...] = docs_of(3, 1 - zh0)
    lax.fori_loop(4, 7, step_c(zh0), 0)
    total = d_own[...]
    for m in range(3):
        d_copy(m).wait_recv()
        total = total + d_in[m].astype(F32)
    d_out[3] = total.astype(BF16)
    d_copy(Z_COPY).start()
    d_own[...] = docs_of(7, zh0)

    mine = jnp.where(lax.rem(y0 + z0, 2) == 0, 3, 7)
    gq_ref[...] = part[mine]
    for k in range(4):
        for z in range(2):
            slot = 2 * k + z

            def add(slot=slot):
                q_copy_in = pltpu.make_async_remote_copy(
                    src_ref=q_out.at[0], dst_ref=q_in.at[slot],
                    send_sem=q_ss.at[0], recv_sem=q_rs.at[slot],
                    device_id=(qi, lax.rem(ti + 2, 16)), device_id_type=MESH,
                )
                q_copy_in.wait_recv()
                gq_ref[...] += q_in[slot].astype(F32)

            if k < 3:
                add()
            else:
                pl.when(z != z0)(add)
    total = d_own[...]
    for m in (Z_COPY, 4, 5, 6):
        d_copy(m).wait_recv()
        total = total + d_in[3 if m is Z_COPY else m].astype(F32)
    gd_ref[0] = total

    for half in range(2):
        for k in range(1, 16):
            lse_copy(half, k).wait_send()
    for st in range(8):
        pair_copy(st).wait_send()

        @pl.when(is_remote(st))
        def _():
            q_copy(st).wait_send()

    for m in (0, 1, 2, Z_COPY, 4, 5, 6):
        d_copy(m).wait_send()


def put_out(gq_in, gd_in, gq_out, gd_out, sems):
    copies = [pltpu.make_async_copy(gq_in, gq_out, sems.at[0]), pltpu.make_async_copy(gd_in, gd_out, sems.at[1])]
    for copy in copies:
        copy.start()
    for copy in copies:
        copy.wait()


def shards(queries, documents, cotangent):
    vmem = pl.BlockSpec(memory_space=pltpu.VMEM)
    anywhere = pl.BlockSpec(memory_space=pl.ANY)
    dma = pltpu.SemaphoreType.DMA
    n_docs = documents.shape[0]
    grads = pl.pallas_call(
        kernel,
        out_shape=(
            pltpu.VMEM((BLK, DIM), F32),
            pltpu.VMEM((1, BLK, DIM), F32),
        ),
        in_specs=[anywhere, anywhere, pl.BlockSpec(memory_space=pltpu.SMEM)],
        out_specs=(vmem, vmem),
        scratch_shapes=[
            pltpu.VMEM(queries.shape, BF16),
            pltpu.VMEM(documents.shape, BF16),
            dma((2,)),
            pltpu.VMEM((NBLK, n_docs, BLK), F32),
            pltpu.VMEM((NBLK, n_docs, BLK), BF16),
            pltpu.VMEM((n_docs, 2 * DIM), BF16),
            pltpu.VMEM((DIM, n_docs), BF16),
            pltpu.VMEM((NBLK, BLK), F32),
            pltpu.VMEM((2, 8, BLK), F32),
            pltpu.VMEM((2, 15, 8, BLK), F32),
            pltpu.VMEM((NBLK, BLK), F32),
            pltpu.VMEM((8, BLK, DIM), F32),
            pltpu.VMEM((8, BLK, DIM), F32),
            pltpu.VMEM((8, BLK, DIM), F32),
            pltpu.VMEM((8, BLK, DIM), BF16),
            pltpu.VMEM((8, BLK, DIM), BF16),
            pltpu.VMEM((7, BLK, DIM), BF16),
            pltpu.VMEM((7, BLK, DIM), BF16),
            pltpu.VMEM((BLK, DIM), F32),
            dma((2, 15)), dma((2, 15)), dma((8,)), dma((8,)),
            dma((8,)), dma((8,)), dma((7,)), dma((7,)),
        ],
        compiler_params=pltpu.CompilerParams(
            collective_id=0, has_side_effects=True, vmem_limit_bytes=VMEM_LIMIT
        ),
    )(queries, documents, cotangent)
    return pl.pallas_call(
        put_out,
        out_shape=(
            jax.ShapeDtypeStruct((BLK, DIM), F32),
            jax.ShapeDtypeStruct((1, BLK, DIM), F32),
        ),
        in_specs=[vmem, vmem],
        out_specs=(anywhere, anywhere),
        scratch_shapes=[dma((2,))],
    )(*(pltpu.with_memory_space_constraint(g, pltpu.VMEM) for g in grads))


def solution(mesh):
    placed = (P("query", None), P("tok", None), P("query"))
    return jax.shard_map(
        shards,
        mesh=mesh,
        in_specs=placed,
        out_specs=(P(("query", "tok"), None), P("tok", "query", None)),
        check_vma=False,
    )
```

```python
import functools

import jax
import jax.numpy as jnp
from jax import lax
from jax.experimental import pallas as pl
from jax.experimental.pallas import tpu as pltpu
from jax.sharding import PartitionSpec as P

QLEN = 32
inv_temp = 2.0
LOG2E = 1.4426950408889634
SCALE = inv_temp * LOG2E

MESH = pl.DeviceIdType.MESH
F32 = jnp.float32
BF16 = jnp.bfloat16

BLK = 256
NBLK = 16
NDBLK = 8
DIM = 128
CHUNK = 256
NCHUNK = 8
SUBROWS = 16
Z_COPY = None
VMEM_LIMIT = 62 * 2**20


def block_of(slot):
    half, rest = slot // 8, lax.rem(slot, 8)
    y, core = rest // 2, lax.rem(rest, 2)
    return 4 * y + 2 * lax.rem(half + y, 2) + core


def kernel(
    q_ref, d_ref, cot_ref, gq_ref, gd_ref,
    s_ref, u_ref, dc_ref, dt_ref, w_ref, lse_mine, lse_all, lse_ref,
    pair_out, pair_in, part, q_out, q_in, d_part, d_out, d_in, d_own,
    lse_ss, lse_rs, pair_ss, pair_rs, q_ss, q_rs, d_ss, d_rs,
):
    qi, ti = lax.axis_index("query"), lax.axis_index("tok")
    x0, zh0 = qi // 2, lax.rem(qi, 2)
    y0, z0, core = ti // 4, lax.rem(ti // 2, 2), lax.rem(ti, 2)

    barrier = pltpu.get_barrier_semaphore()
    for k in range(1, 16):
        pl.semaphore_signal(barrier, inc=1, device_id=(qi, lax.rem(ti + k, 16)), device_id_type=MESH)
    for k in range(1, 4):
        pl.semaphore_signal(barrier, inc=1, device_id=(2 * lax.rem(x0 + k, 4) + zh0, ti), device_id_type=MESH)
    pl.semaphore_signal(barrier, inc=1, device_id=(2 * x0 + 1 - zh0, ti), device_id_type=MESH)

    for c in range(NCHUNK):
        rows = slice(c * CHUNK, (c + 1) * CHUNK)
        scaled = d_ref[rows, :].astype(F32) * SCALE
        high = scaled.astype(BF16)
        dc_ref[rows, 0:DIM] = high
        dc_ref[rows, DIM : 2 * DIM] = (scaled - high.astype(F32)).astype(BF16)

    def q_pair(slot):
        rows = q_ref[pl.ds(pl.multiple_of(block_of(slot) * BLK, BLK), BLK), :]
        return jnp.concatenate([rows, rows], axis=1)

    def score_chunk(slot, c, q2, tops):
        rows = slice(c * CHUNK, (c + 1) * CHUNK)
        s = lax.dot_general(dc_ref[rows, :], q2, (((1,), (1,)), ((), ())), preferred_element_type=F32)
        s_ref[slot, rows, :] = s
        for i in range(0, CHUNK, SUBROWS):
            part_s = s[i : i + SUBROWS]
            tops = part_s if tops is None else jnp.maximum(tops, part_s)
        return tops

    def exp_chunk(slot, c, top, total):
        for i in range(c * CHUNK, (c + 1) * CHUNK, SUBROWS):
            e = jnp.exp2(s_ref[slot, i : i + SUBROWS, :] - top)
            total = e if total is None else total + e
        return total

    def local_lse(half, row, top, total):
        lse_mine[half, pl.ds(row, 1), :] = top + jnp.log2(jnp.sum(total, axis=0, keepdims=True))

    def scores_of(slot):
        q2 = q_pair(slot)
        tops = None
        for c in range(NCHUNK):
            tops = score_chunk(slot, c, q2, tops)
        return jnp.max(tops, axis=0, keepdims=True)

    def turn(i):
        cols = pl.ds(pl.multiple_of(i * 2 * DIM, 2 * DIM), 2 * DIM)
        dt_ref[:, cols] = d_ref[cols, :].T

    def step_a(half):
        def body(i, tops):
            turn(i)
            new = []
            for k in range(2):
                slot = 2 * i + k
                q2 = q_pair(slot + 2)
                total = fresh = None
                for c in range(NCHUNK):
                    total = exp_chunk(slot, c, tops[k], total)
                    fresh = score_chunk(slot + 2, c, q2, fresh)
                local_lse(half, slot - 8 * half, tops[k], total)
                new.append(jnp.max(fresh, axis=0, keepdims=True))
            return tuple(new)

        return body

    def lse_copy(half, k):
        return pltpu.make_async_remote_copy(
            src_ref=lse_mine.at[half], dst_ref=lse_all.at[half, k - 1],
            send_sem=lse_ss.at[half, k - 1], recv_sem=lse_rs.at[half, k - 1],
            device_id=(qi, lax.rem(ti + k, 16)), device_id_type=MESH,
        )

    tops = lax.fori_loop(0, 4, step_a(0), (scores_of(0), scores_of(1)))
    pl.semaphore_wait(barrier, 19)
    for k in range(1, 16):
        lse_copy(0, k).start()
    tops = lax.fori_loop(4, 7, step_a(1), tops)
    turn(7)
    for k in range(2):
        total = None
        for c in range(NCHUNK):
            total = exp_chunk(14 + k, c, tops[k], total)
        local_lse(1, 6 + k, tops[k], total)
    for k in range(1, 16):
        lse_copy(1, k).start()

    lane_query = lax.broadcasted_iota(jnp.int32, (1, BLK), 1) // QLEN
    for slot in range(NBLK):
        half, y, cb = slot // 8, (slot % 8) // 2, slot % 2
        block = 4 * y + 2 * ((half + y) % 2) + cb
        w = jnp.zeros((1, BLK), F32)
        for g in range(BLK // QLEN):
            w = jnp.where(lane_query == g, cot_ref[block * (BLK // QLEN) + g], w)
        w_ref[slot : slot + 1, :] = w

    def doc_rows(x, zh):
        return pl.ds(pl.multiple_of((2 * x + zh) * BLK, BLK), BLK)

    def query_grads(slot):
        lse = lse_ref[pl.ds(slot, 1), :]
        w = w_ref[pl.ds(slot, 1), :]
        acc = jnp.zeros((DIM, BLK), F32)
        for c in range(NCHUNK):
            rows = slice(c * CHUNK, (c + 1) * CHUNK)
            p = jnp.exp2(s_ref[slot, rows, :] - lse)
            u_ref[slot, rows, :] = (w * p).astype(BF16)
            acc = acc + jnp.dot(dt_ref[:, rows], p.astype(BF16), preferred_element_type=F32)
        return (w * acc).T

    def pair_copy(st):
        return pltpu.make_async_remote_copy(
            src_ref=pair_out.at[st], dst_ref=pair_in.at[st],
            send_sem=pair_ss.at[st], recv_sem=pair_rs.at[st],
            device_id=(qi, ti + 1 - 2 * core), device_id_type=MESH,
        )

    def target(st):
        half, k = st // 4, lax.rem(st, 4)
        y = lax.rem(y0 + 1 + k, 4)
        return k, y, lax.rem(half + y, 2)

    def q_copy(st):
        k, y, z = target(st)
        slot = 2 * k + z0
        return pltpu.make_async_remote_copy(
            src_ref=q_out.at[st], dst_ref=q_in.at[slot],
            send_sem=q_ss.at[st], recv_sem=q_rs.at[slot],
            device_id=(qi, 4 * y + 2 * z + core), device_id_type=MESH,
        )

    def finish(st):
        pair_copy(st).wait_recv()
        both = part[st] + pair_in[st]
        part[st] = both
        q_out[st] = both.astype(BF16)

    def is_remote(st):
        k, y, z = target(st)
        return jnp.logical_or(k != 3, z != z0)

    def send(st):
        @pl.when(is_remote(st))
        def _():
            q_copy(st).start()

    def d_target(m):
        m = lax.rem(m, 4)
        return lax.rem(x0 + jnp.where(m == 2, 3, jnp.where(m == 3, 0, 2 - m)), 4)

    def docs_of(m, zh, slots=range(NBLK), acc=None):
        rows = doc_rows(d_target(m), zh)
        for slot in slots:
            half, y, cb = slot // 8, (slot % 8) // 2, slot % 2
            blk = 4 * y + 2 * ((half + y) % 2) + cb
            term = jnp.dot(u_ref[slot, rows, :], q_ref[blk * BLK : (blk + 1) * BLK, :], preferred_element_type=F32)
            acc = term if acc is None else acc + term
        return acc

    def early_docs(i, _):
        for m in (2 * i, 2 * i + 1):
            d_part[m] = docs_of(m, 1 - zh0, range(8))
        return 0

    def step_b(i, _):
        for st in (2 * i, 2 * i + 1):
            _, y, _ = target(st)
            base = 8 * (st // 4) + 2 * y
            pair_out[st] = query_grads(base + 1 - core)
            part[st] = query_grads(base + core)
        for st in (2 * i, 2 * i + 1):
            pair_copy(st).start()

        @pl.when(i > 0)
        def _():
            for st in (2 * i - 2, 2 * i - 1):
                finish(st)
            for st in (2 * i - 2, 2 * i - 1):
                send(st)

        return 0

    for half in range(2):
        for k in range(1, 16):
            lse_copy(half, k).wait_recv()
        top = lse_mine[half]
        for k in range(15):
            top = jnp.maximum(top, lse_all[half, k])
        total = jnp.exp2(lse_mine[half] - top)
        for k in range(15):
            total = total + jnp.exp2(lse_all[half, k] - top)
        lse_ref[8 * half : 8 * half + 8, :] = top + jnp.log2(total)
        lax.fori_loop(2 * half, 2 * half + 2, step_b, 0)
        if half == 0:
            lax.fori_loop(0, 2, early_docs, 0)

    def d_copy(m):
        device = 2 * x0 + 1 - zh0 if m is Z_COPY else 2 * d_target(m) + zh0
        m = 3 if m is Z_COPY else m
        return pltpu.make_async_remote_copy(
            src_ref=d_out.at[m], dst_ref=d_in.at[m],
            send_sem=d_ss.at[m], recv_sem=d_rs.at[m],
            device_id=(device, ti), device_id_type=MESH,
        )

    def step_cross(m, _):
        d_out[m] = docs_of(m, 1 - zh0, range(8, NBLK), d_part[m]).astype(BF16)
        d_copy(m).start()
        return 0

    def step_same(m, _):
        d_out[m] = docs_of(m, zh0).astype(BF16)
        d_copy(m).start()
        return 0

    lax.fori_loop(0, 3, step_cross, 0)
    for st in (6, 7):
        finish(st)
    for st in (6, 7):
        send(st)
    d_own[...] = docs_of(3, 1 - zh0, range(8, NBLK), d_part[3])
    lax.fori_loop(4, 7, step_same, 0)
    total = d_own[...]
    for m in range(3):
        d_copy(m).wait_recv()
        total = total + d_in[m].astype(F32)
    d_out[3] = total.astype(BF16)
    d_copy(Z_COPY).start()
    d_own[...] = docs_of(7, zh0)

    mine = jnp.where(lax.rem(y0 + z0, 2) == 0, 3, 7)
    gq_ref[...] = part[mine]
    for k in range(4):
        for z in range(2):
            slot = 2 * k + z

            def add(slot=slot):
                q_copy_in = pltpu.make_async_remote_copy(
                    src_ref=q_out.at[0], dst_ref=q_in.at[slot],
                    send_sem=q_ss.at[0], recv_sem=q_rs.at[slot],
                    device_id=(qi, lax.rem(ti + 2, 16)), device_id_type=MESH,
                )
                q_copy_in.wait_recv()
                gq_ref[...] += q_in[slot].astype(F32)

            if k < 3:
                add()
            else:
                pl.when(z != z0)(add)
    total = d_own[...]
    for m in (Z_COPY, 4, 5, 6):
        d_copy(m).wait_recv()
        total = total + d_in[3 if m is Z_COPY else m].astype(F32)
    gd_ref[0] = total

    for half in range(2):
        for k in range(1, 16):
            lse_copy(half, k).wait_send()
    for st in range(8):
        pair_copy(st).wait_send()

        @pl.when(is_remote(st))
        def _():
            q_copy(st).wait_send()

    for m in (0, 1, 2, Z_COPY, 4, 5, 6):
        d_copy(m).wait_send()


def put_out(gq_in, gd_in, gq_out, gd_out, sems):
    copies = [pltpu.make_async_copy(gq_in, gq_out, sems.at[0]), pltpu.make_async_copy(gd_in, gd_out, sems.at[1])]
    for copy in copies:
        copy.start()
    for copy in copies:
        copy.wait()


def shards(queries, documents, cotangent):
    vmem = pl.BlockSpec(memory_space=pltpu.VMEM)
    dma = pltpu.SemaphoreType.DMA
    n_docs = documents.shape[0]
    grads = pl.pallas_call(
        kernel,
        out_shape=(
            pltpu.VMEM((BLK, DIM), F32),
            pltpu.VMEM((1, BLK, DIM), F32),
        ),
        in_specs=[vmem, vmem, pl.BlockSpec(memory_space=pltpu.SMEM)],
        out_specs=(vmem, vmem),
        scratch_shapes=[
            pltpu.VMEM((NBLK, n_docs, BLK), F32),
            pltpu.VMEM((NBLK, n_docs, BLK), BF16),
            pltpu.VMEM((n_docs, 2 * DIM), BF16),
            pltpu.VMEM((DIM, n_docs), BF16),
            pltpu.VMEM((NBLK, BLK), F32),
            pltpu.VMEM((2, 8, BLK), F32),
            pltpu.VMEM((2, 15, 8, BLK), F32),
            pltpu.VMEM((NBLK, BLK), F32),
            pltpu.VMEM((8, BLK, DIM), F32),
            pltpu.VMEM((8, BLK, DIM), F32),
            pltpu.VMEM((8, BLK, DIM), F32),
            pltpu.VMEM((8, BLK, DIM), BF16),
            pltpu.VMEM((8, BLK, DIM), BF16),
            pltpu.VMEM((4, BLK, DIM), F32),
            pltpu.VMEM((7, BLK, DIM), BF16),
            pltpu.VMEM((7, BLK, DIM), BF16),
            pltpu.VMEM((BLK, DIM), F32),
            dma((2, 15)), dma((2, 15)), dma((8,)), dma((8,)),
            dma((8,)), dma((8,)), dma((7,)), dma((7,)),
        ],
        compiler_params=pltpu.CompilerParams(
            collective_id=0, has_side_effects=True, vmem_limit_bytes=VMEM_LIMIT
        ),
    )(queries, documents, cotangent)
    anywhere = pl.BlockSpec(memory_space=pl.ANY)
    return pl.pallas_call(
        put_out,
        out_shape=(
            jax.ShapeDtypeStruct((BLK, DIM), F32),
            jax.ShapeDtypeStruct((1, BLK, DIM), F32),
        ),
        in_specs=[vmem, vmem],
        out_specs=(anywhere, anywhere),
        scratch_shapes=[dma((2,))],
    )(*(pltpu.with_memory_space_constraint(g, pltpu.VMEM) for g in grads))


def solution(mesh):
    placed = (P("query", None), P("tok", None), P("query"))
    return jax.shard_map(
        shards,
        mesh=mesh,
        in_specs=placed,
        out_specs=(P(("query", "tok"), None), P("tok", "query", None)),
        check_vma=False,
    )
```

```python
import functools

import jax
import jax.numpy as jnp
from jax import lax
from jax.experimental import pallas as pl
from jax.experimental.pallas import tpu as pltpu
from jax.sharding import PartitionSpec as P

QLEN = 32
inv_temp = 2.0
LOG2E = 1.4426950408889634
SCALE = inv_temp * LOG2E

MESH = pl.DeviceIdType.MESH
F32 = jnp.float32
BF16 = jnp.bfloat16

BLK = 256
NBLK = 16
NDBLK = 8
DIM = 128
CHUNK = 256
NCHUNK = 8
SUBROWS = 16
Z_COPY = None
VMEM_LIMIT = 62 * 2**20


def block_of(slot):
    half, rest = slot // 8, lax.rem(slot, 8)
    y, core = rest // 2, lax.rem(rest, 2)
    return 4 * y + 2 * lax.rem(half + y, 2) + core


def kernel(
    q_ref, d_ref, cot_ref, gq_ref, gd_ref,
    s_ref, u_ref, dc_ref, dt_ref, w_ref, lse_mine, lse_all, lse_ref,
    pair_out, pair_in, part, q_out, q_in, d_out, d_in, d_own,
    lse_ss, lse_rs, pair_ss, pair_rs, q_ss, q_rs, d_ss, d_rs,
):
    qi, ti = lax.axis_index("query"), lax.axis_index("tok")
    x0, zh0 = qi // 2, lax.rem(qi, 2)
    y0, z0, core = ti // 4, lax.rem(ti // 2, 2), lax.rem(ti, 2)

    barrier = pltpu.get_barrier_semaphore()
    for k in range(1, 16):
        pl.semaphore_signal(barrier, inc=1, device_id=(qi, lax.rem(ti + k, 16)), device_id_type=MESH)
    for k in range(1, 4):
        pl.semaphore_signal(barrier, inc=1, device_id=(2 * lax.rem(x0 + k, 4) + zh0, ti), device_id_type=MESH)
    pl.semaphore_signal(barrier, inc=1, device_id=(2 * x0 + 1 - zh0, ti), device_id_type=MESH)

    for c in range(NCHUNK):
        rows = slice(c * CHUNK, (c + 1) * CHUNK)
        scaled = d_ref[rows, :].astype(F32) * SCALE
        high = scaled.astype(BF16)
        dc_ref[rows, 0:DIM] = high
        dc_ref[rows, DIM : 2 * DIM] = (scaled - high.astype(F32)).astype(BF16)

    lane_query = lax.broadcasted_iota(jnp.int32, (1, BLK), 1) // QLEN
    for slot in range(NBLK):
        half, y, cb = slot // 8, (slot % 8) // 2, slot % 2
        block = 4 * y + 2 * ((half + y) % 2) + cb
        w = jnp.zeros((1, BLK), F32)
        for g in range(BLK // QLEN):
            w = jnp.where(lane_query == g, cot_ref[block * (BLK // QLEN) + g], w)
        w_ref[slot : slot + 1, :] = w

    def q_pair(slot):
        rows = q_ref[pl.ds(pl.multiple_of(block_of(slot) * BLK, BLK), BLK), :]
        return jnp.concatenate([rows, rows], axis=1)

    def score_chunk(slot, c, q2, tops):
        rows = slice(c * CHUNK, (c + 1) * CHUNK)
        s = lax.dot_general(dc_ref[rows, :], q2, (((1,), (1,)), ((), ())), preferred_element_type=F32)
        s_ref[slot, rows, :] = s
        for i in range(0, CHUNK, SUBROWS):
            part_s = s[i : i + SUBROWS]
            tops = part_s if tops is None else jnp.maximum(tops, part_s)
        return tops

    def exp_chunk(slot, c, top, total):
        for i in range(c * CHUNK, (c + 1) * CHUNK, SUBROWS):
            e = jnp.exp2(s_ref[slot, i : i + SUBROWS, :] - top)
            total = e if total is None else total + e
        return total

    def local_lse(half, row, top, total):
        lse_mine[half, pl.ds(row, 1), :] = top + jnp.log2(jnp.sum(total, axis=0, keepdims=True))

    def scores_of(slot):
        q2 = q_pair(slot)
        tops = None
        for c in range(NCHUNK):
            tops = score_chunk(slot, c, q2, tops)
        return jnp.max(tops, axis=0, keepdims=True)

    def turn(i):
        cols = pl.ds(pl.multiple_of(i * 2 * DIM, 2 * DIM), 2 * DIM)
        dt_ref[:, cols] = d_ref[cols, :].T

    def step_a(half):
        def body(i, tops):
            turn(i)
            new = []
            for k in range(2):
                slot = 2 * i + k
                q2 = q_pair(slot + 2)
                total = fresh = None
                for c in range(NCHUNK):
                    total = exp_chunk(slot, c, tops[k], total)
                    fresh = score_chunk(slot + 2, c, q2, fresh)
                local_lse(half, slot - 8 * half, tops[k], total)
                new.append(jnp.max(fresh, axis=0, keepdims=True))
            return tuple(new)

        return body

    def lse_copy(half, k):
        return pltpu.make_async_remote_copy(
            src_ref=lse_mine.at[half], dst_ref=lse_all.at[half, k - 1],
            send_sem=lse_ss.at[half, k - 1], recv_sem=lse_rs.at[half, k - 1],
            device_id=(qi, lax.rem(ti + k, 16)), device_id_type=MESH,
        )

    tops = lax.fori_loop(0, 4, step_a(0), (scores_of(0), scores_of(1)))
    pl.semaphore_wait(barrier, 19)
    for k in range(1, 16):
        lse_copy(0, k).start()
    tops = lax.fori_loop(4, 7, step_a(1), tops)
    turn(7)
    for k in range(2):
        total = None
        for c in range(NCHUNK):
            total = exp_chunk(14 + k, c, tops[k], total)
        local_lse(1, 6 + k, tops[k], total)
    for k in range(1, 16):
        lse_copy(1, k).start()

    def doc_rows(x, zh):
        return pl.ds(pl.multiple_of((2 * x + zh) * BLK, BLK), BLK)

    def query_grads(slot):
        lse = lse_ref[pl.ds(slot, 1), :]
        w = w_ref[pl.ds(slot, 1), :]
        acc = jnp.zeros((DIM, BLK), F32)
        for c in range(NCHUNK):
            rows = slice(c * CHUNK, (c + 1) * CHUNK)
            p = jnp.exp2(s_ref[slot, rows, :] - lse)
            u_ref[slot, rows, :] = (w * p).astype(BF16)
            acc = acc + jnp.dot(dt_ref[:, rows], p.astype(BF16), preferred_element_type=F32)
        return (w * acc).T

    def pair_copy(st):
        return pltpu.make_async_remote_copy(
            src_ref=pair_out.at[st], dst_ref=pair_in.at[st],
            send_sem=pair_ss.at[st], recv_sem=pair_rs.at[st],
            device_id=(qi, ti + 1 - 2 * core), device_id_type=MESH,
        )

    def target(st):
        half, k = st // 4, lax.rem(st, 4)
        y = lax.rem(y0 + 1 + k, 4)
        return k, y, lax.rem(half + y, 2)

    def q_copy(st):
        k, y, z = target(st)
        slot = 2 * k + z0
        return pltpu.make_async_remote_copy(
            src_ref=q_out.at[st], dst_ref=q_in.at[slot],
            send_sem=q_ss.at[st], recv_sem=q_rs.at[slot],
            device_id=(qi, 4 * y + 2 * z + core), device_id_type=MESH,
        )

    def finish(st):
        pair_copy(st).wait_recv()
        both = part[st] + pair_in[st]
        part[st] = both
        q_out[st] = both.astype(BF16)

    def is_remote(st):
        k, y, z = target(st)
        return jnp.logical_or(k != 3, z != z0)

    def send(st):
        @pl.when(is_remote(st))
        def _():
            q_copy(st).start()

    def step_b(i, _):
        for st in (2 * i, 2 * i + 1):
            _, y, _ = target(st)
            base = 8 * (st // 4) + 2 * y
            pair_out[st] = query_grads(base + 1 - core)
            part[st] = query_grads(base + core)
        for st in (2 * i, 2 * i + 1):
            pair_copy(st).start()

        @pl.when(i > 0)
        def _():
            for st in (2 * i - 2, 2 * i - 1):
                finish(st)
            for st in (2 * i - 2, 2 * i - 1):
                send(st)

        return 0

    for half in range(2):
        for k in range(1, 16):
            lse_copy(half, k).wait_recv()
        top = lse_mine[half]
        for k in range(15):
            top = jnp.maximum(top, lse_all[half, k])
        total = jnp.exp2(lse_mine[half] - top)
        for k in range(15):
            total = total + jnp.exp2(lse_all[half, k] - top)
        lse_ref[8 * half : 8 * half + 8, :] = top + jnp.log2(total)
        lax.fori_loop(2 * half, 2 * half + 2, step_b, 0)

    def d_target(m):
        m = lax.rem(m, 4)
        return lax.rem(x0 + jnp.where(m == 2, 3, jnp.where(m == 3, 0, 2 - m)), 4)

    def d_copy(m):
        device = 2 * x0 + 1 - zh0 if m is Z_COPY else 2 * d_target(m) + zh0
        m = 3 if m is Z_COPY else m
        return pltpu.make_async_remote_copy(
            src_ref=d_out.at[m], dst_ref=d_in.at[m],
            send_sem=d_ss.at[m], recv_sem=d_rs.at[m],
            device_id=(device, ti), device_id_type=MESH,
        )

    def docs_of(m, zh):
        rows = doc_rows(d_target(m), zh)
        acc = jnp.zeros((BLK, DIM), F32)
        for slot in range(NBLK):
            half, y, cb = slot // 8, (slot % 8) // 2, slot % 2
            blk = 4 * y + 2 * ((half + y) % 2) + cb
            acc = acc + jnp.dot(
                u_ref[slot, rows, :], q_ref[blk * BLK : (blk + 1) * BLK, :], preferred_element_type=F32
            )
        return acc

    def step_c(zh):
        def body(m, _):
            d_out[m] = docs_of(m, zh).astype(BF16)
            d_copy(m).start()
            return 0

        return body

    lax.fori_loop(0, 1, step_c(1 - zh0), 0)
    for st in (6, 7):
        finish(st)
    for st in (6, 7):
        send(st)
    lax.fori_loop(1, 3, step_c(1 - zh0), 0)
    d_own[...] = docs_of(3, 1 - zh0)
    lax.fori_loop(4, 7, step_c(zh0), 0)
    total = d_own[...]
    for m in range(3):
        d_copy(m).wait_recv()
        total = total + d_in[m].astype(F32)
    d_out[3] = total.astype(BF16)
    d_copy(Z_COPY).start()
    d_own[...] = docs_of(7, zh0)

    mine = jnp.where(lax.rem(y0 + z0, 2) == 0, 3, 7)
    gq_ref[...] = part[mine]
    for k in range(4):
        for z in range(2):
            slot = 2 * k + z

            def add(slot=slot):
                q_copy_in = pltpu.make_async_remote_copy(
                    src_ref=q_out.at[0], dst_ref=q_in.at[slot],
                    send_sem=q_ss.at[0], recv_sem=q_rs.at[slot],
                    device_id=(qi, lax.rem(ti + 2, 16)), device_id_type=MESH,
                )
                q_copy_in.wait_recv()
                gq_ref[...] += q_in[slot].astype(F32)

            if k < 3:
                add()
            else:
                pl.when(z != z0)(add)
    total = d_own[...]
    for m in (Z_COPY, 4, 5, 6):
        d_copy(m).wait_recv()
        total = total + d_in[3 if m is Z_COPY else m].astype(F32)
    gd_ref[0] = total

    for half in range(2):
        for k in range(1, 16):
            lse_copy(half, k).wait_send()
    for st in range(8):
        pair_copy(st).wait_send()

        @pl.when(is_remote(st))
        def _():
            q_copy(st).wait_send()

    for m in (0, 1, 2, Z_COPY, 4, 5, 6):
        d_copy(m).wait_send()


def put_out(gq_in, gd_in, gq_out, gd_out, sems):
    copies = [pltpu.make_async_copy(gq_in, gq_out, sems.at[0]), pltpu.make_async_copy(gd_in, gd_out, sems.at[1])]
    for copy in copies:
        copy.start()
    for copy in copies:
        copy.wait()


def shards(queries, documents, cotangent):
    vmem = pl.BlockSpec(memory_space=pltpu.VMEM)
    dma = pltpu.SemaphoreType.DMA
    n_docs = documents.shape[0]
    grads = pl.pallas_call(
        kernel,
        out_shape=(
            pltpu.VMEM((BLK, DIM), F32),
            pltpu.VMEM((1, BLK, DIM), F32),
        ),
        in_specs=[vmem, vmem, pl.BlockSpec(memory_space=pltpu.SMEM)],
        out_specs=(vmem, vmem),
        scratch_shapes=[
            pltpu.VMEM((NBLK, n_docs, BLK), F32),
            pltpu.VMEM((NBLK, n_docs, BLK), BF16),
            pltpu.VMEM((n_docs, 2 * DIM), BF16),
            pltpu.VMEM((DIM, n_docs), BF16),
            pltpu.VMEM((NBLK, BLK), F32),
            pltpu.VMEM((2, 8, BLK), F32),
            pltpu.VMEM((2, 15, 8, BLK), F32),
            pltpu.VMEM((NBLK, BLK), F32),
            pltpu.VMEM((8, BLK, DIM), F32),
            pltpu.VMEM((8, BLK, DIM), F32),
            pltpu.VMEM((8, BLK, DIM), F32),
            pltpu.VMEM((8, BLK, DIM), BF16),
            pltpu.VMEM((8, BLK, DIM), BF16),
            pltpu.VMEM((7, BLK, DIM), BF16),
            pltpu.VMEM((7, BLK, DIM), BF16),
            pltpu.VMEM((BLK, DIM), F32),
            dma((2, 15)), dma((2, 15)), dma((8,)), dma((8,)),
            dma((8,)), dma((8,)), dma((7,)), dma((7,)),
        ],
        compiler_params=pltpu.CompilerParams(
            collective_id=0, has_side_effects=True, vmem_limit_bytes=VMEM_LIMIT,
        ),
    )(queries, documents, cotangent)
    anywhere = pl.BlockSpec(memory_space=pl.ANY)
    return pl.pallas_call(
        put_out,
        out_shape=(
            jax.ShapeDtypeStruct((BLK, DIM), F32),
            jax.ShapeDtypeStruct((1, BLK, DIM), F32),
        ),
        in_specs=[vmem, vmem],
        out_specs=(anywhere, anywhere),
        scratch_shapes=[dma((2,))],
    )(*(pltpu.with_memory_space_constraint(g, pltpu.VMEM) for g in grads))


def solution(mesh):
    placed = (P("query", None), P("tok", None), P("query"))
    return jax.shard_map(
        shards,
        mesh=mesh,
        in_specs=placed,
        out_specs=(P(("query", "tok"), None), P("tok", "query", None)),
        check_vma=False,
    )
```

```python
import functools

import jax
import jax.numpy as jnp
from jax import lax
from jax.experimental import pallas as pl
from jax.experimental.pallas import tpu as pltpu
from jax.sharding import PartitionSpec as P

QLEN = 32
inv_temp = 2.0
LOG2E = 1.4426950408889634
SCALE = inv_temp * LOG2E

MESH = pl.DeviceIdType.MESH
F32 = jnp.float32
BF16 = jnp.bfloat16

BLK = 256
NBLK = 16
NDBLK = 8
DIM = 128
CHUNK = 256
NCHUNK = 8
SUBROWS = 16
Z_COPY = None
VMEM_LIMIT = 62 * 2**20


def block_of(slot):
    half, rest = slot // 8, lax.rem(slot, 8)
    y, core = rest // 2, lax.rem(rest, 2)
    return 4 * y + 2 * lax.rem(half + y, 2) + core


def kernel(
    q_ref, d_ref, cot_ref, gq_ref, gd_ref,
    s_ref, u_ref, dc_ref, dt_ref, w_ref, lse_mine, lse_all, lse_ref,
    pair_out, pair_in, part, q_out, q_in, d_out, d_in, d_own,
    lse_ss, lse_rs, pair_ss, pair_rs, q_ss, q_rs, d_ss, d_rs,
):
    qi, ti = lax.axis_index("query"), lax.axis_index("tok")
    x0, zh0 = qi // 2, lax.rem(qi, 2)
    y0, z0, core = ti // 4, lax.rem(ti // 2, 2), lax.rem(ti, 2)

    barrier = pltpu.get_barrier_semaphore()
    for k in range(1, 16):
        pl.semaphore_signal(barrier, inc=1, device_id=(qi, lax.rem(ti + k, 16)), device_id_type=MESH)
    for k in range(1, 4):
        pl.semaphore_signal(barrier, inc=1, device_id=(2 * lax.rem(x0 + k, 4) + zh0, ti), device_id_type=MESH)
    pl.semaphore_signal(barrier, inc=1, device_id=(2 * x0 + 1 - zh0, ti), device_id_type=MESH)

    for c in range(NCHUNK):
        rows = slice(c * CHUNK, (c + 1) * CHUNK)
        scaled = d_ref[rows, :].astype(F32) * SCALE
        high = scaled.astype(BF16)
        dc_ref[rows, 0:DIM] = high
        dc_ref[rows, DIM : 2 * DIM] = (scaled - high.astype(F32)).astype(BF16)

    def q_pair(slot):
        rows = q_ref[pl.ds(pl.multiple_of(block_of(slot) * BLK, BLK), BLK), :]
        return jnp.concatenate([rows, rows], axis=1)

    def score_chunk(slot, c, q2, tops):
        rows = slice(c * CHUNK, (c + 1) * CHUNK)
        s = lax.dot_general(dc_ref[rows, :], q2, (((1,), (1,)), ((), ())), preferred_element_type=F32)
        s_ref[slot, rows, :] = s
        for i in range(0, CHUNK, SUBROWS):
            part_s = s[i : i + SUBROWS]
            tops = part_s if tops is None else jnp.maximum(tops, part_s)
        return tops

    def exp_chunk(slot, c, top, total):
        for i in range(c * CHUNK, (c + 1) * CHUNK, SUBROWS):
            e = jnp.exp2(s_ref[slot, i : i + SUBROWS, :] - top)
            total = e if total is None else total + e
        return total

    def local_lse(half, row, top, total):
        lse_mine[half, pl.ds(row, 1), :] = top + jnp.log2(jnp.sum(total, axis=0, keepdims=True))

    def scores_of(slot):
        q2 = q_pair(slot)
        tops = None
        for c in range(NCHUNK):
            tops = score_chunk(slot, c, q2, tops)
        return jnp.max(tops, axis=0, keepdims=True)

    def turn(i):
        cols = pl.ds(pl.multiple_of(i * 2 * DIM, 2 * DIM), 2 * DIM)
        dt_ref[:, cols] = d_ref[cols, :].T

    def step_a(half):
        def body(i, tops):
            turn(i)
            new = []
            for k in range(2):
                slot = 2 * i + k
                q2 = q_pair(slot + 2)
                total = fresh = None
                for c in range(NCHUNK):
                    total = exp_chunk(slot, c, tops[k], total)
                    fresh = score_chunk(slot + 2, c, q2, fresh)
                local_lse(half, slot - 8 * half, tops[k], total)
                new.append(jnp.max(fresh, axis=0, keepdims=True))
            return tuple(new)

        return body

    def lse_copy(half, k):
        return pltpu.make_async_remote_copy(
            src_ref=lse_mine.at[half], dst_ref=lse_all.at[half, k - 1],
            send_sem=lse_ss.at[half, k - 1], recv_sem=lse_rs.at[half, k - 1],
            device_id=(qi, lax.rem(ti + k, 16)), device_id_type=MESH,
        )

    tops = lax.fori_loop(0, 4, step_a(0), (scores_of(0), scores_of(1)))
    pl.semaphore_wait(barrier, 19)
    for k in range(1, 16):
        lse_copy(0, k).start()
    tops = lax.fori_loop(4, 7, step_a(1), tops)
    turn(7)
    for k in range(2):
        total = None
        for c in range(NCHUNK):
            total = exp_chunk(14 + k, c, tops[k], total)
        local_lse(1, 6 + k, tops[k], total)
    for k in range(1, 16):
        lse_copy(1, k).start()

    lane_query = lax.broadcasted_iota(jnp.int32, (1, BLK), 1) // QLEN
    for slot in range(NBLK):
        half, y, cb = slot // 8, (slot % 8) // 2, slot % 2
        block = 4 * y + 2 * ((half + y) % 2) + cb
        w = jnp.zeros((1, BLK), F32)
        for g in range(BLK // QLEN):
            w = jnp.where(lane_query == g, cot_ref[block * (BLK // QLEN) + g], w)
        w_ref[slot : slot + 1, :] = w

    def doc_rows(x, zh):
        return pl.ds(pl.multiple_of((2 * x + zh) * BLK, BLK), BLK)

    def query_grads(slot):
        lse = lse_ref[pl.ds(slot, 1), :]
        w = w_ref[pl.ds(slot, 1), :]
        acc = jnp.zeros((DIM, BLK), F32)
        for c in range(NCHUNK):
            rows = slice(c * CHUNK, (c + 1) * CHUNK)
            p = jnp.exp2(s_ref[slot, rows, :] - lse)
            u_ref[slot, rows, :] = (w * p).astype(BF16)
            acc = acc + jnp.dot(dt_ref[:, rows], p.astype(BF16), preferred_element_type=F32)
        return (w * acc).T

    def pair_copy(st):
        return pltpu.make_async_remote_copy(
            src_ref=pair_out.at[st], dst_ref=pair_in.at[st],
            send_sem=pair_ss.at[st], recv_sem=pair_rs.at[st],
            device_id=(qi, ti + 1 - 2 * core), device_id_type=MESH,
        )

    def target(st):
        half, k = st // 4, lax.rem(st, 4)
        y = lax.rem(y0 + 1 + k, 4)
        return k, y, lax.rem(half + y, 2)

    def q_copy(st):
        k, y, z = target(st)
        slot = 2 * k + z0
        return pltpu.make_async_remote_copy(
            src_ref=q_out.at[st], dst_ref=q_in.at[slot],
            send_sem=q_ss.at[st], recv_sem=q_rs.at[slot],
            device_id=(qi, 4 * y + 2 * z + core), device_id_type=MESH,
        )

    def finish(st):
        pair_copy(st).wait_recv()
        both = part[st] + pair_in[st]
        part[st] = both
        q_out[st] = both.astype(BF16)

    def is_remote(st):
        k, y, z = target(st)
        return jnp.logical_or(k != 3, z != z0)

    def send(st):
        @pl.when(is_remote(st))
        def _():
            q_copy(st).start()

    def step_b(i, _):
        for st in (2 * i, 2 * i + 1):
            _, y, _ = target(st)
            base = 8 * (st // 4) + 2 * y
            pair_out[st] = query_grads(base + 1 - core)
            part[st] = query_grads(base + core)
        for st in (2 * i, 2 * i + 1):
            pair_copy(st).start()

        @pl.when(i > 0)
        def _():
            for st in (2 * i - 2, 2 * i - 1):
                finish(st)
            for st in (2 * i - 2, 2 * i - 1):
                send(st)

        return 0

    for half in range(2):
        for k in range(1, 16):
            lse_copy(half, k).wait_recv()
        top = lse_mine[half]
        for k in range(15):
            top = jnp.maximum(top, lse_all[half, k])
        total = jnp.exp2(lse_mine[half] - top)
        for k in range(15):
            total = total + jnp.exp2(lse_all[half, k] - top)
        lse_ref[8 * half : 8 * half + 8, :] = top + jnp.log2(total)
        lax.fori_loop(2 * half, 2 * half + 2, step_b, 0)

    def d_target(m):
        m = lax.rem(m, 4)
        return lax.rem(x0 + jnp.where(m == 2, 3, jnp.where(m == 3, 0, 2 - m)), 4)

    def d_copy(m):
        device = 2 * x0 + 1 - zh0 if m is Z_COPY else 2 * d_target(m) + zh0
        m = 3 if m is Z_COPY else m
        return pltpu.make_async_remote_copy(
            src_ref=d_out.at[m], dst_ref=d_in.at[m],
            send_sem=d_ss.at[m], recv_sem=d_rs.at[m],
            device_id=(device, ti), device_id_type=MESH,
        )

    def docs_of(m, zh):
        rows = doc_rows(d_target(m), zh)
        acc = jnp.zeros((BLK, DIM), F32)
        for slot in range(NBLK):
            half, y, cb = slot // 8, (slot % 8) // 2, slot % 2
            blk = 4 * y + 2 * ((half + y) % 2) + cb
            acc = acc + jnp.dot(
                u_ref[slot, rows, :], q_ref[blk * BLK : (blk + 1) * BLK, :], preferred_element_type=F32
            )
        return acc

    def step_c(zh):
        def body(m, _):
            d_out[m] = docs_of(m, zh).astype(BF16)
            d_copy(m).start()
            return 0

        return body

    lax.fori_loop(0, 1, step_c(1 - zh0), 0)
    for st in (6, 7):
        finish(st)
    for st in (6, 7):
        send(st)
    lax.fori_loop(1, 3, step_c(1 - zh0), 0)
    d_own[...] = docs_of(3, 1 - zh0)
    lax.fori_loop(4, 6, step_c(zh0), 0)
    total = d_own[...]
    for m in range(3):
        d_copy(m).wait_recv()
        total = total + d_in[m].astype(F32)
    d_out[3] = total.astype(BF16)
    d_copy(Z_COPY).start()
    lax.fori_loop(6, 7, step_c(zh0), 0)
    d_own[...] = docs_of(7, zh0)

    mine = jnp.where(lax.rem(y0 + z0, 2) == 0, 3, 7)
    gq_ref[...] = part[mine]
    for k in range(4):
        for z in range(2):
            slot = 2 * k + z

            def add(slot=slot):
                q_copy_in = pltpu.make_async_remote_copy(
                    src_ref=q_out.at[0], dst_ref=q_in.at[slot],
                    send_sem=q_ss.at[0], recv_sem=q_rs.at[slot],
                    device_id=(qi, lax.rem(ti + 2, 16)), device_id_type=MESH,
                )
                q_copy_in.wait_recv()
                gq_ref[...] += q_in[slot].astype(F32)

            if k < 3:
                add()
            else:
                pl.when(z != z0)(add)
    total = d_own[...]
    for m in (Z_COPY, 4, 5, 6):
        d_copy(m).wait_recv()
        total = total + d_in[3 if m is Z_COPY else m].astype(F32)
    gd_ref[0] = total

    for half in range(2):
        for k in range(1, 16):
            lse_copy(half, k).wait_send()
    for st in range(8):
        pair_copy(st).wait_send()

        @pl.when(is_remote(st))
        def _():
            q_copy(st).wait_send()

    for m in (0, 1, 2, Z_COPY, 4, 5, 6):
        d_copy(m).wait_send()


def put_out(gq_in, gd_in, gq_out, gd_out, sems):
    copies = [pltpu.make_async_copy(gq_in, gq_out, sems.at[0]), pltpu.make_async_copy(gd_in, gd_out, sems.at[1])]
    for copy in copies:
        copy.start()
    for copy in copies:
        copy.wait()


def shards(queries, documents, cotangent):
    vmem = pl.BlockSpec(memory_space=pltpu.VMEM)
    dma = pltpu.SemaphoreType.DMA
    n_docs = documents.shape[0]
    grads = pl.pallas_call(
        kernel,
        out_shape=(
            pltpu.VMEM((BLK, DIM), F32),
            pltpu.VMEM((1, BLK, DIM), F32),
        ),
        in_specs=[vmem, vmem, pl.BlockSpec(memory_space=pltpu.SMEM)],
        out_specs=(vmem, vmem),
        scratch_shapes=[
            pltpu.VMEM((NBLK, n_docs, BLK), F32),
            pltpu.VMEM((NBLK, n_docs, BLK), BF16),
            pltpu.VMEM((n_docs, 2 * DIM), BF16),
            pltpu.VMEM((DIM, n_docs), BF16),
            pltpu.VMEM((NBLK, BLK), F32),
            pltpu.VMEM((2, 8, BLK), F32),
            pltpu.VMEM((2, 15, 8, BLK), F32),
            pltpu.VMEM((NBLK, BLK), F32),
            pltpu.VMEM((8, BLK, DIM), F32),
            pltpu.VMEM((8, BLK, DIM), F32),
            pltpu.VMEM((8, BLK, DIM), F32),
            pltpu.VMEM((8, BLK, DIM), BF16),
            pltpu.VMEM((8, BLK, DIM), BF16),
            pltpu.VMEM((7, BLK, DIM), BF16),
            pltpu.VMEM((7, BLK, DIM), BF16),
            pltpu.VMEM((BLK, DIM), F32),
            dma((2, 15)), dma((2, 15)), dma((8,)), dma((8,)),
            dma((8,)), dma((8,)), dma((7,)), dma((7,)),
        ],
        compiler_params=pltpu.CompilerParams(
            collective_id=0, has_side_effects=True, vmem_limit_bytes=VMEM_LIMIT
        ),
    )(queries, documents, cotangent)
    anywhere = pl.BlockSpec(memory_space=pl.ANY)
    return pl.pallas_call(
        put_out,
        out_shape=(
            jax.ShapeDtypeStruct((BLK, DIM), F32),
            jax.ShapeDtypeStruct((1, BLK, DIM), F32),
        ),
        in_specs=[vmem, vmem],
        out_specs=(anywhere, anywhere),
        scratch_shapes=[dma((2,))],
    )(*(pltpu.with_memory_space_constraint(g, pltpu.VMEM) for g in grads))


def solution(mesh):
    placed = (P("query", None), P("tok", None), P("query"))
    return jax.shard_map(
        shards,
        mesh=mesh,
        in_specs=placed,
        out_specs=(P(("query", "tok"), None), P("tok", "query", None)),
        check_vma=False,
    )
```
